256 devices in a mesh: sta: 8 (over x, y_lo), tm: 32 (over z, y_hi, core).
Axes of the slice: x: 4, y: 4 (y_hi: 2, y_lo: 2; y = y_hi * 2 + y_lo), z: 8, core: 2. Of those that a mesh axis runs over, the one named last changes fastest.
Arguments:
- record: bfloat16 [16, 3, 16384], P('sta', None, 'tm'), may hold values from -6 to 6
- templates: bfloat16 [16, 256, 768], P('sta'), may hold values from -6 to 6
- moveouts: int32 [16, 256], P('sta'), may hold values from 0 to 255
- live_mask: int32 [16], P('sta'), may hold values 0 or 1
- owner_order: int32 [256], replicated, may hold values from 0 to 255, each once
Outputs:
- detection: float32 [256, 16384], P('sta', 'tm')
The draws below stay inside these ranges and needn't reach their ends.
All inputs are finite; a program needn't handle non-finite values. No bound on the sum of `live_mask` on one device may be relied on, other than what follows from the above.
Results may differ from the reference program's by a relative error of at most 0.0029.
Values may be sent and summed in bfloat16 or wider, within the bound.
No kernel may reach another device: no remote copies, remote signals or barrier semaphores. Data moves between devices by JAX's collectives and lax.ppermute only.
A program may use at most 64 MiB of HBM per device.

```python
import math
import jax
import jax.numpy as jnp
from jax import lax

K = 256
TLEN = 256
COMPS = 3
MAXM = 256
NSTA = 16
SAMPLES = 16384


def plant(array, stream_key, smallest, top_value):
    extent = array.shape
    spot = [jax.random.randint(jax.random.fold_in(stream_key, axis), (), 0, extent[axis]) for axis in range(len(extent))]
    array = array.at[tuple(spot)].set(smallest)
    longest = extent.index(max(extent))
    spot[longest] = (spot[longest] + 1) % extent[longest]
    return array.at[tuple(spot)].set(top_value)


def shard_levels(own_key, dims, cuts, least, high):
    gain = 1.0
    for axis_at, parts in cuts:
        steps = jax.random.uniform(jax.random.fold_in(jax.random.fold_in(own_key, 6), axis_at), (parts,), jnp.float32, least / len(cuts), high / len(cuts))
        gain = gain * jnp.repeat(jnp.exp(steps), dims[axis_at] // parts).reshape((-1,) + (1,) * (len(dims) - 1 - axis_at))
    return gain


def gaussian(rng, shape, scale, reach, cuts=(), kind=jnp.bfloat16):
    factor_of = shard_levels(rng, shape, cuts, -0.22, 0.18) if cuts else 1.0
    values = jax.random.normal(rng, shape, jnp.float32) * scale * factor_of
    return jnp.minimum(jnp.maximum(values, -reach), reach).astype(kind)


def setup_inputs(seed: int = 0) -> dict:
    splits = jax.random.split(jax.random.key(seed), 6)
    record = gaussian(splits[0], (NSTA, COMPS, SAMPLES), 1.0, 6.0, ((0, 8), (2, 32)))
    templates = gaussian(splits[1], (NSTA, K, COMPS * TLEN), 1.0, 6.0, ((0, 8),))
    moveouts = plant(jax.random.randint(splits[2], (NSTA, K), 0, MAXM), jax.random.fold_in(splits[2], 1), 0, MAXM - 1).astype(jnp.int32)
    live_mask = plant((jax.random.randint(splits[3], (NSTA,), 0, 8) < 7).astype(jnp.int32), jax.random.fold_in(splits[3], 1), 0, 1)
    owner_order = jax.random.permutation(splits[4], K).astype(jnp.int32)
    return {"record": record, "templates": templates, "moveouts": moveouts, "live_mask": live_mask, "owner_order": owner_order}


epsilon = 1e-05

def normalized(record_one, template_one, columns):
    squares = lax.optimization_barrier(jnp.sum(jnp.square(record_one.astype(jnp.float32)), axis=0))
    window_sums = lax.reduce_window(squares, jnp.float32(0.0), lax.add, (TLEN,), (1,), 'VALID')
    energy = window_sums[:columns]
    record_rms = jnp.sqrt(energy / (COMPS * TLEN) + epsilon)
    template_rms = jnp.sqrt(lax.optimization_barrier(jnp.mean(jnp.square(template_one.astype(jnp.float32)), axis=-1)) + epsilon)
    kernel = template_one.reshape(K, COMPS, TLEN)
    correlation = lax.conv_general_dilated(record_one[None], kernel, (1,), 'VALID', preferred_element_type=jnp.float32)[0, :, :columns]
    return (correlation / (COMPS * TLEN * record_rms[None, :] * template_rms[:, None])).astype(jnp.bfloat16)

def reference(record, templates, moveouts, live_mask, owner_order):
    extended = jnp.pad(record, ((0, 0), (0, 0), (0, TLEN + MAXM)))

    def station(running_sum, station_items):
        record_one, template_one, shift_one, live_one = station_items
        ncc = normalized(record_one, template_one, SAMPLES + MAXM)
        places = jnp.arange(SAMPLES, dtype=jnp.int32)[None, :] + shift_one[:, None]
        picked = jnp.take_along_axis(ncc, places, axis=1)
        return (running_sum + picked.astype(jnp.float32) * live_one.astype(jnp.float32), None)
    start_sum = jnp.zeros((K, SAMPLES), jnp.float32)
    running_sum, unused = lax.scan(station, start_sum, (extended, templates, moveouts, live_mask))
    return running_sum[owner_order] * math.sqrt(COMPS * TLEN / NSTA)
```

```python
import math

import jax
import jax.numpy as jnp
from jax import lax
from jax.experimental import pallas as pl
from jax.experimental.pallas import tpu as pltpu
from jax.sharding import PartitionSpec as P

TLEN = 256
MAXM = 256
LANES = 128
PACK = 16


epsilon = 1e-05


def column_of(row, size):
    here = lax.broadcasted_iota(jnp.int32, (size, size), 0)
    there = lax.broadcasted_iota(jnp.int32, (size, size), 1)
    return jnp.sum(jnp.where(here == there, row, jnp.zeros_like(row)), axis=1, keepdims=True)


def stack_kernel(live_ref, own_ref, next_ref, template_ref, moveout_ref, order_ref, out_ref, frames_ref):
    components, stations, block = own_ref.shape
    kcount, taps = template_ref.shape[1:]
    columns = block + MAXM
    span = 2 * block
    lane = lax.broadcasted_iota(jnp.int32, (kcount, LANES), 1)
    total = jnp.zeros((kcount, block), jnp.float32)
    for s in range(stations):
        squares = jnp.zeros((1, span), jnp.float32)
        for c in range(components):
            signal = jnp.concatenate([own_ref[c, s : s + 1, :], next_ref[c, s : s + 1, :]], axis=1).astype(jnp.float32)
            squares = squares + signal * signal
            base = jnp.concatenate(
                [pltpu.roll(signal, span - r, 1) if r else signal for r in range(PACK)], axis=0
            )
            for q in range(LANES // PACK):
                moved = pltpu.roll(base, span - q * PACK, 1) if q else base
                moved = moved[:, : columns + LANES].astype(jnp.bfloat16)
                for h in range(TLEN // LANES):
                    start = c * TLEN + h * LANES + q * PACK
                    frames_ref[start : start + PACK, :] = moved[:, h * LANES : h * LANES + columns]
        energy = squares
        step = 1
        while step < TLEN:
            energy = energy + pltpu.roll(energy, span - step, 1)
            step *= 2
        record_scale = 1.0 / (taps * jnp.sqrt(energy[:, :columns] / taps + epsilon))
        weights = template_ref[s]
        wide = weights.astype(jnp.float32)
        template_scale = 1.0 / jnp.sqrt(jnp.sum(wide * wide, axis=1, keepdims=True) / taps + epsilon)
        correlation = jnp.dot(weights, frames_ref[...], preferred_element_type=jnp.float32)
        scores = (correlation * record_scale * template_scale).astype(jnp.bfloat16).astype(jnp.float32)
        moveout = column_of(moveout_ref[s : s + 1, :], kcount)
        low = moveout % LANES
        place = lane + low
        inside = place < LANES
        place = place % LANES
        far = moveout >= LANES
        turned = [
            jnp.take_along_axis(scores[:, i * LANES : (i + 1) * LANES], place, axis=1)
            for i in range(columns // LANES)
        ]
        near = [jnp.where(inside, turned[i], turned[i + 1]) for i in range(columns // LANES - 1)]
        picked = jnp.concatenate([jnp.where(far, near[i + 1], near[i]) for i in range(block // LANES)], axis=1)
        total = total + picked * live_ref[s].astype(jnp.float32)
    order = column_of(order_ref[...], kcount)
    chosen = order == lax.broadcasted_iota(jnp.int32, (kcount, kcount), 1)
    rows = jnp.dot(
        chosen.astype(jnp.bfloat16), total.astype(jnp.bfloat16), preferred_element_type=jnp.float32
    )
    out_ref[...] = rows.astype(jnp.bfloat16).reshape(out_ref.shape)


def shards(record, templates, moveouts, live_mask, owner_order):
    stations, components, block = record.shape
    kcount, taps = templates.shape[1:]
    count = lax.axis_size("tm")
    groups = lax.axis_size("sta")
    own = jnp.transpose(record, (1, 0, 2))
    ahead = lax.ppermute(own, "tm", [(source, source - 1) for source in range(1, count)])
    vmem = pl.BlockSpec(memory_space=pltpu.VMEM)
    partial = pl.pallas_call(
        stack_kernel,
        out_shape=jax.ShapeDtypeStruct((groups, kcount // groups, block), jnp.bfloat16),
        in_specs=[pl.BlockSpec(memory_space=pltpu.SMEM), vmem, vmem, vmem, vmem, vmem],
        out_specs=vmem,
        scratch_shapes=[pltpu.VMEM((taps, block + MAXM), jnp.bfloat16)],
        compiler_params=pltpu.CompilerParams(vmem_limit_bytes=40 << 20),
        name="stack",
    )(live_mask, own, ahead, templates, moveouts, owner_order.reshape(1, kcount))
    parts = lax.all_to_all(partial, "sta", 0, 0)
    stack_scale = math.sqrt(components * TLEN / (stations * groups))
    return jnp.sum(parts.astype(jnp.float32), axis=0) * stack_scale


def solution(mesh):
    placed = (P("sta", None, "tm"), P("sta", None, None), P("sta", None), P("sta"), P())
    return jax.shard_map(
        shards, mesh=mesh, in_specs=placed, out_specs=P("sta", "tm"), check_vma=False
    )
```

```python
import math

import jax
import jax.numpy as jnp
from jax import lax
from jax.experimental import pallas as pl
from jax.experimental.pallas import tpu as pltpu
from jax.sharding import PartitionSpec as P
TLEN = 256
MAXM = 256
LANES = 128
SPAN = 16
epsilon = 1e-05


def column_of(row, size):
    here = lax.broadcasted_iota(jnp.int32, (size, size), 0)
    there = lax.broadcasted_iota(jnp.int32, (size, size), 1)
    return jnp.sum(jnp.where(here == there, row, jnp.zeros_like(row)), axis=1, keepdims=True)


def block_of(array, i):
    return array[:, i * LANES : (i + 1) * LANES]


def backwards(ref, blocks):
    components, stations = ref.shape[:2]
    rows = jnp.concatenate([ref[c].astype(jnp.float32) for c in range(components)], axis=0)
    rows = jnp.concatenate([rows, jnp.zeros((-rows.shape[0] % 8, rows.shape[1]), jnp.float32)], axis=0)
    mirror = LANES - 1 - lax.broadcasted_iota(jnp.int32, (rows.shape[0], LANES), 1)
    return [jnp.take_along_axis(block_of(rows, i), mirror, axis=1) for i in reversed(blocks)]


def staircase(row, count, step):
    return pltpu.roll(jnp.broadcast_to(row, (count, row.shape[1])), 0, 1, stride=step, stride_axis=0)


def record_scale_of(rows, stations, s, taps):
    squares = sum(jnp.square(rows[r : r + 1]) for r in range(s, taps // TLEN * stations, stations))
    energy = jnp.sum(staircase(squares, SPAN, 1), axis=0, keepdims=True)
    energy = jnp.sum(staircase(energy, LANES // SPAN, SPAN), axis=0, keepdims=True)
    energy = energy + pltpu.roll(energy, LANES, 1)
    return 1.0 / (taps * jnp.sqrt(energy / taps + epsilon))


def lag(moveout):
    return lax.broadcasted_iota(jnp.int32, moveout.shape, 1) + (moveout & (LANES - 1))


def turn(correlation, record_scale, template_scale, reach):
    score = (correlation * record_scale * template_scale).astype(jnp.bfloat16).astype(jnp.float32)
    return jnp.take_along_axis(score, LANES - 1 - (reach & (LANES - 1)), axis=1)


def near_kernel(
    live_ref, own_ref, template_ref, moveout_ref, order_ref,
    factor_ref, scale_ref, delay_ref, chosen_ref, corner_ref, joined_ref, turned_ref, frames_ref, *, gain
):
    components, stations, block = own_ref.shape
    kcount, taps = template_ref.shape[1:]
    rows = jnp.concatenate(backwards(own_ref, range(block // LANES)), axis=1)
    last = block // LANES - 1
    for s in range(stations):
        for c in range(components):
            r = c * stations + s
            steps = staircase(rows[r : r + 1], LANES, 1).astype(jnp.bfloat16)
            corner_ref[s, c * LANES : (c + 1) * LANES, :] = block_of(steps, last - 2)
            for h in range(TLEN // LANES):
                start = c * TLEN + h * LANES
                frames_ref[s, start : start + LANES, :] = steps[:, (last - 1 - h) * LANES : (last + 1 - h) * LANES]
        record_scale = record_scale_of(rows, stations, s, taps)
        wide = template_ref[s].astype(jnp.float32)
        energy = jnp.sum(wide * wide, axis=1, keepdims=True)
        scale = jnp.broadcast_to(1.0 / jnp.sqrt(energy / taps + epsilon), (kcount, LANES))
        scale_ref[s] = scale
        moveout = jnp.broadcast_to(column_of(moveout_ref[s : s + 1, :], kcount), (kcount, LANES))
        delay_ref[s] = moveout
        correlation = jnp.dot(template_ref[s], frames_ref[s], preferred_element_type=jnp.float32)
        reach = lag(moveout)
        first = turn(block_of(correlation, 1), block_of(record_scale, last), scale, reach)
        second = turn(block_of(correlation, 0), block_of(record_scale, last - 1), scale, reach)
        joined_ref[s] = jnp.where(reach < LANES, first, second)
        turned_ref[s] = second
        factor_ref[s] = jnp.broadcast_to(live_ref[0:1, s : s + 1].astype(jnp.float32) * gain, (8, LANES))
    order = column_of(order_ref[...], kcount)
    chosen_ref[...] = (order == lax.broadcasted_iota(jnp.int32, (kcount, kcount), 1)).astype(jnp.bfloat16)


def stack_kernel(
    own_ref, next_ref, template_ref, factor_ref, scale_ref, delay_ref, chosen_ref, corner_ref, joined_ref, turned_ref,
    out_ref, frames_ref
):
    components, stations, block = own_ref.shape
    kcount, taps = template_ref.shape[1:]
    count = block // LANES
    rows = jnp.concatenate(
        backwards(next_ref, range(count)) + backwards(own_ref, range(count - 2, count)), axis=1
    )
    total = [jnp.zeros((kcount, LANES), jnp.float32) for _ in range(count)]
    for s in range(stations):
        for c in range(components):
            r = c * stations + s
            steps = staircase(rows[r : r + 1, : (count + 1) * LANES], LANES, 1).astype(jnp.bfloat16)
            start = c * TLEN
            frames_ref[s, start : start + LANES, : (count - 1) * LANES] = steps[:, 2 * LANES :]
            frames_ref[s, start : start + LANES, (count - 1) * LANES :] = corner_ref[s, c * LANES : (c + 1) * LANES, :]
            frames_ref[s, start + LANES : start + TLEN, :] = steps[:, LANES:]
    for s in range(stations):
        record_scale = record_scale_of(rows, stations, s, taps)
        correlation = jnp.dot(template_ref[s], frames_ref[s], preferred_element_type=jnp.float32)
        moveout = delay_ref[s]
        reach = lag(moveout)
        far = moveout >= LANES
        factor = factor_ref[s, 0:1]
        turned = [turned_ref[s]] + [
            turn(block_of(correlation, i), block_of(record_scale, 2 + i), scale_ref[s], reach)
            for i in reversed(range(count))
        ]
        joined = [joined_ref[s]] + [jnp.where(reach < LANES, turned[i], turned[i + 1]) for i in range(count)]
        for i in range(count):
            total[i] = total[i] + jnp.where(far, joined[i + 1], joined[i]) * factor
    stacked = jnp.concatenate(total, axis=1).astype(jnp.bfloat16)
    placed = jnp.dot(chosen_ref[...], stacked, preferred_element_type=jnp.float32)
    out_ref[...] = placed.astype(jnp.bfloat16).reshape(out_ref.shape)


def near_part(own, templates, moveouts, live_mask, owner_order, gain):
    components, stations, block = own.shape
    kcount, taps = templates.shape[1:]
    vmem = pl.BlockSpec(memory_space=pltpu.VMEM)
    row = (stations, kcount, LANES)
    shapes = [
        ((stations, 8, LANES), jnp.float32), (row, jnp.float32), (row, jnp.int32), ((kcount, kcount), jnp.bfloat16),
        ((stations, taps // 2, LANES), jnp.bfloat16), (row, jnp.float32), (row, jnp.float32),
    ]
    return pl.pallas_call(
        lambda *refs: near_kernel(*refs, gain=gain),
        out_shape=[jax.ShapeDtypeStruct(*shape) for shape in shapes],
        in_specs=[vmem] * 5,
        out_specs=[vmem] * len(shapes),
        scratch_shapes=[pltpu.VMEM((stations, taps, 2 * LANES), jnp.bfloat16)],
        compiler_params=pltpu.CompilerParams(vmem_limit_bytes=32 << 20),
        name="near",
    )(live_mask.reshape(1, stations), own, templates, moveouts, owner_order.reshape(1, kcount))


def stack_part(own, ahead, templates, near, groups):
    components, stations, block = own.shape
    kcount, taps = templates.shape[1:]
    vmem = pl.BlockSpec(memory_space=pltpu.VMEM)
    return pl.pallas_call(
        stack_kernel,
        out_shape=jax.ShapeDtypeStruct((groups, kcount // groups, block), jnp.bfloat16),
        in_specs=[vmem] * (3 + len(near)),
        out_specs=vmem,
        scratch_shapes=[pltpu.VMEM((stations, taps, block), jnp.bfloat16)],
        compiler_params=pltpu.CompilerParams(vmem_limit_bytes=32 << 20),
        name="stack",
    )(own, ahead, templates, *near)


def shards(record, templates, moveouts, live_mask, owner_order):
    stations, components = record.shape[:2]
    count = lax.axis_size("tm")
    groups = lax.axis_size("sta")
    own = jnp.transpose(record, (1, 0, 2))
    ahead = lax.ppermute(own, "tm", [(source, source - 1) for source in range(1, count)])
    gain = math.sqrt(components * TLEN / (stations * groups))
    near = near_part(own, templates, moveouts, live_mask, owner_order, gain)
    partial = stack_part(own, ahead, templates, near, groups)
    parts = lax.all_to_all(partial, "sta", 0, 0)
    return jnp.sum(parts.astype(jnp.float32), axis=0)


def solution(mesh):
    placed = (P("sta", None, "tm"), P("sta", None, None), P("sta", None), P("sta"), P())
    return jax.shard_map(
        shards, mesh=mesh, in_specs=placed, out_specs=P("sta", "tm"), check_vma=False
    )
```

```python
import math

import jax
import jax.numpy as jnp
from jax import lax
from jax.experimental import pallas as pl
from jax.experimental.pallas import tpu as pltpu
from jax.sharding import PartitionSpec as P
TLEN = 256
MAXM = 256
LANES = 128
SPAN = 16
epsilon = 1e-05


def column_of(row, size):
    here = lax.broadcasted_iota(jnp.int32, (size, size), 0)
    there = lax.broadcasted_iota(jnp.int32, (size, size), 1)
    return jnp.sum(jnp.where(here == there, row, jnp.zeros_like(row)), axis=1, keepdims=True)


def block_of(array, i):
    return array[:, i * LANES : (i + 1) * LANES]


def backwards(ref, blocks):
    components, stations = ref.shape[:2]
    rows = jnp.concatenate([ref[c].astype(jnp.float32) for c in range(components)], axis=0)
    rows = jnp.concatenate([rows, jnp.zeros((-rows.shape[0] % 8, rows.shape[1]), jnp.float32)], axis=0)
    mirror = LANES - 1 - lax.broadcasted_iota(jnp.int32, (rows.shape[0], LANES), 1)
    return [jnp.take_along_axis(block_of(rows, i), mirror, axis=1) for i in reversed(blocks)]


def staircase(row, count, step):
    return pltpu.roll(jnp.broadcast_to(row, (count, row.shape[1])), 0, 1, stride=step, stride_axis=0)


def record_scale_of(rows, stations, s, taps):
    squares = sum(jnp.square(rows[r : r + 1]) for r in range(s, taps // TLEN * stations, stations))
    energy = jnp.sum(staircase(squares, SPAN, 1), axis=0, keepdims=True)
    energy = jnp.sum(staircase(energy, LANES // SPAN, SPAN), axis=0, keepdims=True)
    energy = energy + pltpu.roll(energy, LANES, 1)
    return 1.0 / (taps * jnp.sqrt(energy / taps + epsilon))


def lag(moveout):
    return lax.broadcasted_iota(jnp.int32, moveout.shape, 1) + (moveout & (LANES - 1))


def turn(correlation, record_scale, template_scale, reach):
    score = (correlation * record_scale * template_scale).astype(jnp.bfloat16).astype(jnp.float32)
    return jnp.take_along_axis(score, LANES - 1 - (reach & (LANES - 1)), axis=1)


def near_kernel(
    live_hbm, own_hbm, template_hbm, moveout_hbm, order_hbm,
    template_ref, tail_ref, factor_ref, scale_ref, delay_ref, chosen_ref, corner_ref, joined_ref, turned_ref,
    live_ref, own_ref, moveout_ref, order_ref, frames_ref, small_sem, template_sem, *, gain
):
    components, stations, block = own_ref.shape
    kcount, taps = template_ref.shape[1:]
    pairs = [(own_hbm, own_ref), (moveout_hbm, moveout_ref), (order_hbm, order_ref), (live_hbm, live_ref)]
    small = [pltpu.make_async_copy(*pair, small_sem.at[i]) for i, pair in enumerate(pairs)]
    large = [
        pltpu.make_async_copy(template_hbm.at[s], template_ref.at[s], template_sem.at[s]) for s in range(stations)
    ]
    for copy in small + large:
        copy.start()
    small[0].wait()
    blocks = backwards(own_ref, range(block // LANES))
    rows = jnp.concatenate(blocks, axis=1)
    last = block // LANES - 1
    for i in range(2):
        tail_ref[:, i * LANES : (i + 1) * LANES] = blocks[i]
    for s in range(stations):
        for c in range(components):
            r = c * stations + s
            steps = staircase(rows[r : r + 1], LANES, 1).astype(jnp.bfloat16)
            corner_ref[s, c * LANES : (c + 1) * LANES, :] = block_of(steps, last - 2)
            for h in range(TLEN // LANES):
                start = c * TLEN + h * LANES
                frames_ref[s, start : start + LANES, :] = steps[:, (last - 1 - h) * LANES : (last + 1 - h) * LANES]
    for copy in small[1:]:
        copy.wait()
    order = column_of(order_ref[...], kcount)
    chosen_ref[...] = (order == lax.broadcasted_iota(jnp.int32, (kcount, kcount), 1)).astype(jnp.bfloat16)
    for s in range(stations):
        delay_ref[s] = jnp.broadcast_to(column_of(moveout_ref[s : s + 1, :], kcount), (kcount, LANES))
        factor_ref[s] = jnp.broadcast_to(live_ref[0:1, s : s + 1].astype(jnp.float32) * gain, (8, LANES))
    for s in range(stations):
        large[s].wait()
        record_scale = record_scale_of(rows, stations, s, taps)
        wide = template_ref[s].astype(jnp.float32)
        energy = jnp.sum(wide * wide, axis=1, keepdims=True)
        scale = jnp.broadcast_to(1.0 / jnp.sqrt(energy / taps + epsilon), (kcount, LANES))
        scale_ref[s] = scale
        correlation = jnp.dot(template_ref[s], frames_ref[s], preferred_element_type=jnp.float32)
        reach = lag(delay_ref[s])
        first = turn(block_of(correlation, 1), block_of(record_scale, last), scale, reach)
        second = turn(block_of(correlation, 0), block_of(record_scale, last - 1), scale, reach)
        joined_ref[s] = jnp.where(reach < LANES, first, second)
        turned_ref[s] = second


def stack_kernel(
    next_ref, template_ref, tail_ref, factor_ref, scale_ref, delay_ref, chosen_ref, corner_ref, joined_ref, turned_ref,
    out_ref, frames_ref
):
    components, stations, block = next_ref.shape
    kcount, taps = template_ref.shape[1:]
    count = block // LANES
    rows = jnp.concatenate(backwards(next_ref, range(count)) + [tail_ref[...]], axis=1)
    total = [jnp.zeros((kcount, LANES), jnp.float32) for _ in range(count)]
    for s in range(stations):
        for c in range(components):
            r = c * stations + s
            steps = staircase(rows[r : r + 1, : (count + 1) * LANES], LANES, 1).astype(jnp.bfloat16)
            start = c * TLEN
            frames_ref[s, start : start + LANES, : (count - 1) * LANES] = steps[:, 2 * LANES :]
            frames_ref[s, start : start + LANES, (count - 1) * LANES :] = corner_ref[s, c * LANES : (c + 1) * LANES, :]
            frames_ref[s, start + LANES : start + TLEN, :] = steps[:, LANES:]
    for s in range(stations):
        record_scale = record_scale_of(rows, stations, s, taps)
        correlation = jnp.dot(template_ref[s], frames_ref[s], preferred_element_type=jnp.float32)
        moveout = delay_ref[s]
        reach = lag(moveout)
        far = moveout >= LANES
        factor = factor_ref[s, 0:1]
        turned = [turned_ref[s]] + [
            turn(block_of(correlation, i), block_of(record_scale, 2 + i), scale_ref[s], reach)
            for i in reversed(range(count))
        ]
        joined = [joined_ref[s]] + [jnp.where(reach < LANES, turned[i], turned[i + 1]) for i in range(count)]
        for i in range(count):
            total[i] = total[i] + jnp.where(far, joined[i + 1], joined[i]) * factor
    stacked = jnp.concatenate(total, axis=1).astype(jnp.bfloat16)
    placed = jnp.dot(chosen_ref[...], stacked, preferred_element_type=jnp.float32)
    out_ref[...] = placed.astype(jnp.bfloat16).reshape(out_ref.shape)


def near_part(own, templates, moveouts, live_mask, owner_order, gain):
    components, stations, block = own.shape
    kcount, taps = templates.shape[1:]
    row = (stations, kcount, LANES)
    shapes = [
        (templates.shape, jnp.bfloat16), ((-(-components * stations // 8) * 8, 2 * LANES), jnp.float32),
        ((stations, 8, LANES), jnp.float32), (row, jnp.float32), (row, jnp.int32), ((kcount, kcount), jnp.bfloat16),
        ((stations, taps // 2, LANES), jnp.bfloat16), (row, jnp.float32), (row, jnp.float32),
    ]
    return pl.pallas_call(
        lambda *refs: near_kernel(*refs, gain=gain),
        out_shape=[jax.ShapeDtypeStruct(*shape) for shape in shapes],
        in_specs=[pl.BlockSpec(memory_space=pltpu.HBM)] * 5,
        out_specs=[pl.BlockSpec(memory_space=pltpu.VMEM)] * len(shapes),
        scratch_shapes=[
            pltpu.VMEM((1, stations), jnp.int32),
            pltpu.VMEM(own.shape, own.dtype),
            pltpu.VMEM(moveouts.shape, moveouts.dtype),
            pltpu.VMEM((1, kcount), jnp.int32),
            pltpu.VMEM((stations, taps, 2 * LANES), jnp.bfloat16),
            pltpu.SemaphoreType.DMA((4,)),
            pltpu.SemaphoreType.DMA((stations,)),
        ],
        compiler_params=pltpu.CompilerParams(vmem_limit_bytes=32 << 20),
        name="near",
    )(*(
        pltpu.with_memory_space_constraint(operand, pltpu.HBM)
        for operand in (live_mask.reshape(1, stations), own, templates, moveouts, owner_order.reshape(1, kcount))
    ))


def stack_part(ahead, near, groups):
    components, stations, block = ahead.shape
    kcount, taps = near[0].shape[1:]
    vmem = pl.BlockSpec(memory_space=pltpu.VMEM)
    return pl.pallas_call(
        stack_kernel,
        out_shape=jax.ShapeDtypeStruct((groups, kcount // groups, block), jnp.bfloat16),
        in_specs=[vmem] * (1 + len(near)),
        out_specs=vmem,
        scratch_shapes=[pltpu.VMEM((stations, taps, block), jnp.bfloat16)],
        compiler_params=pltpu.CompilerParams(vmem_limit_bytes=32 << 20),
        name="stack",
    )(ahead, *near)


def shards(record, templates, moveouts, live_mask, owner_order):
    stations, components = record.shape[:2]
    count = lax.axis_size("tm")
    groups = lax.axis_size("sta")
    own = jnp.transpose(record, (1, 0, 2))
    ahead = lax.ppermute(own, "tm", [(source, source - 1) for source in range(1, count)])
    gain = math.sqrt(components * TLEN / (stations * groups))
    near = near_part(own, templates, moveouts, live_mask, owner_order, gain)
    partial = stack_part(ahead, near, groups)
    parts = lax.all_to_all(partial, "sta", 0, 0)
    return jnp.sum(parts.astype(jnp.float32), axis=0)


def solution(mesh):
    placed = (P("sta", None, "tm"), P("sta", None, None), P("sta", None), P("sta"), P())
    return jax.shard_map(
        shards, mesh=mesh, in_specs=placed, out_specs=P("sta", "tm"), check_vma=False
    )
```

```python
import math

import jax
import jax.numpy as jnp
from jax import lax
from jax.experimental import pallas as pl
from jax.experimental.pallas import tpu as pltpu
from jax.sharding import PartitionSpec as P
TLEN = 256
MAXM = 256
LANES = 128
SPAN = 16
epsilon = 1e-05


def column_of(row, size):
    here = lax.broadcasted_iota(jnp.int32, (size, size), 0)
    there = lax.broadcasted_iota(jnp.int32, (size, size), 1)
    return jnp.sum(jnp.where(here == there, row, jnp.zeros_like(row)), axis=1, keepdims=True)


def block_of(array, i):
    return array[:, i * LANES : (i + 1) * LANES]


def backwards(ref, blocks):
    components, stations = ref.shape[:2]
    rows = jnp.concatenate([ref[c].astype(jnp.float32) for c in range(components)], axis=0)
    rows = jnp.concatenate([rows, jnp.zeros((-rows.shape[0] % 8, rows.shape[1]), jnp.float32)], axis=0)
    mirror = LANES - 1 - lax.broadcasted_iota(jnp.int32, (rows.shape[0], LANES), 1)
    return [jnp.take_along_axis(block_of(rows, i), mirror, axis=1) for i in reversed(blocks)]


def staircase(row, count, step):
    return pltpu.roll(jnp.broadcast_to(row, (count, row.shape[1])), 0, 1, stride=step, stride_axis=0)


def record_scale_of(rows, stations, s, taps):
    squares = sum(jnp.square(rows[r : r + 1]) for r in range(s, taps // TLEN * stations, stations))
    energy = jnp.sum(staircase(squares, SPAN, 1), axis=0, keepdims=True)
    energy = jnp.sum(staircase(energy, LANES // SPAN, SPAN), axis=0, keepdims=True)
    energy = energy + pltpu.roll(energy, LANES, 1)
    return 1.0 / (taps * jnp.sqrt(energy / taps + epsilon))


def lag(moveout):
    return lax.broadcasted_iota(jnp.int32, moveout.shape, 1) + (moveout & (LANES - 1))


def turn(correlation, record_scale, template_scale, reach):
    score = (correlation * record_scale * template_scale).astype(jnp.bfloat16).astype(jnp.float32)
    return jnp.take_along_axis(score, LANES - 1 - (reach & (LANES - 1)), axis=1)


def near_kernel(
    live_hbm, own_hbm, template_hbm, moveout_hbm, order_hbm,
    placed_ref, tail_ref, factor_ref, scale_ref, delay_ref, corner_ref, joined_ref, turned_ref,
    template_ref, live_ref, own_ref, moveout_ref, order_ref, frames_ref, sems, *, gain
):
    components, stations, block = own_ref.shape
    kcount, taps = template_ref.shape[1:]
    pairs = [
        (own_hbm, own_ref), (moveout_hbm, moveout_ref), (order_hbm, order_ref), (live_hbm, live_ref),
        (template_hbm, template_ref),
    ]
    copies = [pltpu.make_async_copy(*pair, sems.at[i]) for i, pair in enumerate(pairs)]
    for copy in copies:
        copy.start()
    for copy in copies[:-1]:
        copy.wait()
    blocks = backwards(own_ref, range(block // LANES))
    rows = jnp.concatenate(blocks, axis=1)
    last = block // LANES - 1
    for i in range(2):
        tail_ref[:, i * LANES : (i + 1) * LANES] = blocks[i]
    for s in range(stations):
        for c in range(components):
            r = c * stations + s
            steps = staircase(rows[r : r + 1], LANES, 1).astype(jnp.bfloat16)
            corner_ref[s, c * LANES : (c + 1) * LANES, :] = block_of(steps, last - 2)
            for h in range(TLEN // LANES):
                start = c * TLEN + h * LANES
                frames_ref[s, start : start + LANES, :] = steps[:, (last - 1 - h) * LANES : (last + 1 - h) * LANES]
    order = column_of(order_ref[...], kcount)
    chosen = (order == lax.broadcasted_iota(jnp.int32, (kcount, kcount), 1)).astype(jnp.bfloat16)
    delays = lax.dot_general(
        chosen, moveout_ref[...].astype(jnp.bfloat16), (((1,), (1,)), ((), ())), preferred_element_type=jnp.float32
    ).astype(jnp.int32)
    for s in range(stations):
        delay_ref[s] = jnp.broadcast_to(delays[:, s : s + 1], (kcount, LANES))
        factor_ref[s] = jnp.broadcast_to(live_ref[0:1, s : s + 1].astype(jnp.float32) * gain, (8, LANES))
    copies[-1].wait()
    for s in range(stations):
        record_scale = record_scale_of(rows, stations, s, taps)
        wide = jnp.dot(chosen, template_ref[s], preferred_element_type=jnp.float32)
        placed_ref[s] = wide.astype(jnp.bfloat16)
        energy = jnp.sum(wide * wide, axis=1, keepdims=True)
        scale = jnp.broadcast_to(1.0 / jnp.sqrt(energy / taps + epsilon), (kcount, LANES))
        scale_ref[s] = scale
        correlation = jnp.dot(placed_ref[s], frames_ref[s], preferred_element_type=jnp.float32)
        reach = lag(delay_ref[s])
        first = turn(block_of(correlation, 1), block_of(record_scale, last), scale, reach)
        second = turn(block_of(correlation, 0), block_of(record_scale, last - 1), scale, reach)
        joined_ref[s] = jnp.where(reach < LANES, first, second)
        turned_ref[s] = second


def stack_kernel(
    next_ref, placed_ref, tail_ref, factor_ref, scale_ref, delay_ref, corner_ref, joined_ref, turned_ref,
    out_ref, frames_ref
):
    components, stations, block = next_ref.shape
    kcount, taps = placed_ref.shape[1:]
    count = block // LANES
    rows = jnp.concatenate(backwards(next_ref, range(count)) + [tail_ref[...]], axis=1)
    total = [jnp.zeros((kcount, LANES), jnp.float32) for _ in range(count)]
    for s in range(stations):
        for c in range(components):
            r = c * stations + s
            steps = staircase(rows[r : r + 1, : (count + 1) * LANES], LANES, 1).astype(jnp.bfloat16)
            start = c * TLEN
            frames_ref[s, start : start + LANES, : (count - 1) * LANES] = steps[:, 2 * LANES :]
            frames_ref[s, start : start + LANES, (count - 1) * LANES :] = corner_ref[s, c * LANES : (c + 1) * LANES, :]
            frames_ref[s, start + LANES : start + TLEN, :] = steps[:, LANES:]
    for s in range(stations):
        record_scale = record_scale_of(rows, stations, s, taps)
        correlation = jnp.dot(placed_ref[s], frames_ref[s], preferred_element_type=jnp.float32)
        moveout = delay_ref[s]
        reach = lag(moveout)
        far = moveout >= LANES
        factor = factor_ref[s, 0:1]
        turned = [turned_ref[s]] + [
            turn(block_of(correlation, i), block_of(record_scale, 2 + i), scale_ref[s], reach)
            for i in reversed(range(count))
        ]
        joined = [joined_ref[s]] + [jnp.where(reach < LANES, turned[i], turned[i + 1]) for i in range(count)]
        for i in range(count):
            total[i] = total[i] + jnp.where(far, joined[i + 1], joined[i]) * factor
    out_ref[...] = jnp.concatenate(total, axis=1).astype(jnp.bfloat16).reshape(out_ref.shape)


def near_part(own, templates, moveouts, live_mask, owner_order, gain):
    components, stations, block = own.shape
    kcount, taps = templates.shape[1:]
    row = (stations, kcount, LANES)
    shapes = [
        (templates.shape, jnp.bfloat16), ((-(-components * stations // 8) * 8, 2 * LANES), jnp.float32),
        ((stations, 8, LANES), jnp.float32), (row, jnp.float32), (row, jnp.int32),
        ((stations, taps // 2, LANES), jnp.bfloat16), (row, jnp.float32), (row, jnp.float32),
    ]
    return pl.pallas_call(
        lambda *refs: near_kernel(*refs, gain=gain),
        out_shape=[jax.ShapeDtypeStruct(*shape) for shape in shapes],
        in_specs=[pl.BlockSpec(memory_space=pltpu.HBM)] * 5,
        out_specs=[pl.BlockSpec(memory_space=pltpu.VMEM)] * len(shapes),
        scratch_shapes=[
            pltpu.VMEM(templates.shape, templates.dtype),
            pltpu.VMEM((1, stations), jnp.int32),
            pltpu.VMEM(own.shape, own.dtype),
            pltpu.VMEM(moveouts.shape, moveouts.dtype),
            pltpu.VMEM((1, kcount), jnp.int32),
            pltpu.VMEM((stations, taps, 2 * LANES), jnp.bfloat16),
            pltpu.SemaphoreType.DMA((5,)),
        ],
        compiler_params=pltpu.CompilerParams(vmem_limit_bytes=32 << 20),
        name="near",
    )(*(
        pltpu.with_memory_space_constraint(operand, pltpu.HBM)
        for operand in (live_mask.reshape(1, stations), own, templates, moveouts, owner_order.reshape(1, kcount))
    ))


def stack_part(ahead, near, groups):
    components, stations, block = ahead.shape
    kcount, taps = near[0].shape[1:]
    vmem = pl.BlockSpec(memory_space=pltpu.VMEM)
    return pl.pallas_call(
        stack_kernel,
        out_shape=jax.ShapeDtypeStruct((groups, kcount // groups, block), jnp.bfloat16),
        in_specs=[vmem] * (1 + len(near)),
        out_specs=vmem,
        scratch_shapes=[pltpu.VMEM((stations, taps, block), jnp.bfloat16)],
        compiler_params=pltpu.CompilerParams(vmem_limit_bytes=32 << 20),
        name="stack",
    )(ahead, *near)


def shards(record, templates, moveouts, live_mask, owner_order):
    stations, components = record.shape[:2]
    count = lax.axis_size("tm")
    groups = lax.axis_size("sta")
    own = jnp.transpose(record, (1, 0, 2))
    ahead = lax.ppermute(own, "tm", [(source, source - 1) for source in range(1, count)])
    gain = math.sqrt(components * TLEN / (stations * groups))
    near = near_part(own, templates, moveouts, live_mask, owner_order, gain)
    partial = stack_part(ahead, near, groups)
    parts = lax.all_to_all(partial, "sta", 0, 0)
    return jnp.sum(parts.astype(jnp.float32), axis=0)


def solution(mesh):
    placed = (P("sta", None, "tm"), P("sta", None, None), P("sta", None), P("sta"), P())
    return jax.shard_map(
        shards, mesh=mesh, in_specs=placed, out_specs=P("sta", "tm"), check_vma=False
    )
```

```python
import math

import jax
import jax.numpy as jnp
from jax import lax
from jax.experimental import pallas as pl
from jax.experimental.pallas import tpu as pltpu
from jax.sharding import PartitionSpec as P
TLEN = 256
MAXM = 256
LANES = 128
SPAN = 16
epsilon = 1e-05


def column_of(row, size):
    here = lax.broadcasted_iota(jnp.int32, (size, size), 0)
    there = lax.broadcasted_iota(jnp.int32, (size, size), 1)
    return jnp.sum(jnp.where(here == there, row, jnp.zeros_like(row)), axis=1, keepdims=True)


def block_of(array, i):
    return array[:, i * LANES : (i + 1) * LANES]


def backwards(ref, blocks):
    components, stations = ref.shape[:2]
    rows = jnp.concatenate([ref[c].astype(jnp.float32) for c in range(components)], axis=0)
    rows = jnp.concatenate([rows, jnp.zeros((-rows.shape[0] % 8, rows.shape[1]), jnp.float32)], axis=0)
    mirror = LANES - 1 - lax.broadcasted_iota(jnp.int32, (rows.shape[0], LANES), 1)
    return [jnp.take_along_axis(block_of(rows, i), mirror, axis=1) for i in reversed(blocks)]


def staircase(row, count, step):
    return pltpu.roll(jnp.broadcast_to(row, (count, row.shape[1])), 0, 1, stride=step, stride_axis=0)


def record_scale_of(rows, stations, s, taps):
    squares = sum(jnp.square(rows[r : r + 1]) for r in range(s, taps // TLEN * stations, stations))
    energy = jnp.sum(staircase(squares, SPAN, 1), axis=0, keepdims=True)
    energy = jnp.sum(staircase(energy, LANES // SPAN, SPAN), axis=0, keepdims=True)
    energy = energy + pltpu.roll(energy, LANES, 1)
    return 1.0 / (taps * jnp.sqrt(energy / taps + epsilon))


def lag(moveout):
    return lax.broadcasted_iota(jnp.int32, moveout.shape, 1) + (moveout & (LANES - 1))


def turn(correlation, record_scale, template_scale, reach):
    score = (correlation * record_scale * template_scale).astype(jnp.bfloat16).astype(jnp.float32)
    return jnp.take_along_axis(score, LANES - 1 - (reach & (LANES - 1)), axis=1)


def near_kernel(
    live_hbm, own_hbm, template_hbm, moveout_hbm, order_hbm,
    placed_ref, tail_ref, factor_ref, scale_ref, delay_ref, corner_ref, joined_ref, turned_ref,
    template_ref, live_ref, own_ref, moveout_ref, order_ref, frames_ref, sems, *, gain
):
    components, stations, block = own_ref.shape
    kcount, taps = template_ref.shape[1:]
    pairs = [
        (own_hbm, own_ref), (moveout_hbm, moveout_ref), (order_hbm, order_ref), (live_hbm, live_ref),
        (template_hbm, template_ref),
    ]
    copies = [pltpu.make_async_copy(*pair, sems.at[i]) for i, pair in enumerate(pairs)]
    for copy in copies[:1] + copies[2:3] + copies[-1:] + copies[1:2] + copies[3:4]:
        copy.start()
    copies[0].wait()
    copies[2].wait()
    blocks = backwards(own_ref, range(block // LANES))
    rows = jnp.concatenate(blocks, axis=1)
    last = block // LANES - 1
    for i in range(2):
        tail_ref[:, i * LANES : (i + 1) * LANES] = blocks[i]
    for s in range(stations):
        for c in range(components):
            r = c * stations + s
            steps = staircase(rows[r : r + 1], LANES, 1).astype(jnp.bfloat16)
            corner_ref[s, c * LANES : (c + 1) * LANES, :] = block_of(steps, last - 2)
            for h in range(TLEN // LANES):
                start = c * TLEN + h * LANES
                frames_ref[s, start : start + LANES, :] = steps[:, (last - 1 - h) * LANES : (last + 1 - h) * LANES]
    order = column_of(order_ref[...], kcount)
    chosen = (order == lax.broadcasted_iota(jnp.int32, (kcount, kcount), 1)).astype(jnp.bfloat16)
    for copy in (copies[1], copies[3], copies[4]):
        copy.wait()
    delays = lax.dot_general(
        chosen, moveout_ref[...].astype(jnp.bfloat16), (((1,), (1,)), ((), ())), preferred_element_type=jnp.float32
    ).astype(jnp.int32)
    for s in range(stations):
        delay_ref[s] = jnp.broadcast_to(delays[:, s : s + 1], (kcount, LANES))
        factor_ref[s] = jnp.broadcast_to(live_ref[0:1, s : s + 1].astype(jnp.float32) * gain, (8, LANES))
    for s in range(stations):
        record_scale = record_scale_of(rows, stations, s, taps)
        wide = jnp.dot(chosen, template_ref[s], preferred_element_type=jnp.float32)
        placed_ref[s] = wide.astype(jnp.bfloat16)
        energy = jnp.sum(wide * wide, axis=1, keepdims=True)
        scale = jnp.broadcast_to(1.0 / jnp.sqrt(energy / taps + epsilon), (kcount, LANES))
        scale_ref[s] = scale
        correlation = jnp.dot(placed_ref[s], frames_ref[s], preferred_element_type=jnp.float32)
        reach = lag(delay_ref[s])
        first = turn(block_of(correlation, 1), block_of(record_scale, last), scale, reach)
        second = turn(block_of(correlation, 0), block_of(record_scale, last - 1), scale, reach)
        joined_ref[s] = jnp.where(reach < LANES, first, second)
        turned_ref[s] = second


def stack_kernel(
    next_ref, placed_ref, tail_ref, factor_ref, scale_ref, delay_ref, corner_ref, joined_ref, turned_ref,
    out_ref, frames_ref
):
    components, stations, block = next_ref.shape
    kcount, taps = placed_ref.shape[1:]
    count = block // LANES
    rows = jnp.concatenate(backwards(next_ref, range(count)) + [tail_ref[...]], axis=1)
    total = [jnp.zeros((kcount, LANES), jnp.float32) for _ in range(count)]
    for s in range(stations):
        for c in range(components):
            r = c * stations + s
            steps = staircase(rows[r : r + 1, : (count + 1) * LANES], LANES, 1).astype(jnp.bfloat16)
            start = c * TLEN
            frames_ref[s, start : start + LANES, : (count - 1) * LANES] = steps[:, 2 * LANES :]
            frames_ref[s, start : start + LANES, (count - 1) * LANES :] = corner_ref[s, c * LANES : (c + 1) * LANES, :]
            frames_ref[s, start + LANES : start + TLEN, :] = steps[:, LANES:]
    for s in range(stations):
        record_scale = record_scale_of(rows, stations, s, taps)
        correlation = jnp.dot(placed_ref[s], frames_ref[s], preferred_element_type=jnp.float32)
        moveout = delay_ref[s]
        reach = lag(moveout)
        far = moveout >= LANES
        factor = factor_ref[s, 0:1]
        turned = [turned_ref[s]] + [
            turn(block_of(correlation, i), block_of(record_scale, 2 + i), scale_ref[s], reach)
            for i in reversed(range(count))
        ]
        joined = [joined_ref[s]] + [jnp.where(reach < LANES, turned[i], turned[i + 1]) for i in range(count)]
        for i in range(count):
            total[i] = total[i] + jnp.where(far, joined[i + 1], joined[i]) * factor
    out_ref[...] = jnp.concatenate(total, axis=1).astype(jnp.bfloat16).reshape(out_ref.shape)


def near_part(own, templates, moveouts, live_mask, owner_order, gain):
    components, stations, block = own.shape
    kcount, taps = templates.shape[1:]
    row = (stations, kcount, LANES)
    shapes = [
        (templates.shape, jnp.bfloat16), ((-(-components * stations // 8) * 8, 2 * LANES), jnp.float32),
        ((stations, 8, LANES), jnp.float32), (row, jnp.float32), (row, jnp.int32),
        ((stations, taps // 2, LANES), jnp.bfloat16), (row, jnp.float32), (row, jnp.float32),
    ]
    return pl.pallas_call(
        lambda *refs: near_kernel(*refs, gain=gain),
        out_shape=[jax.ShapeDtypeStruct(*shape) for shape in shapes],
        in_specs=[pl.BlockSpec(memory_space=pltpu.HBM)] * 5,
        out_specs=[pl.BlockSpec(memory_space=pltpu.VMEM)] * len(shapes),
        scratch_shapes=[
            pltpu.VMEM(templates.shape, templates.dtype),
            pltpu.VMEM((1, stations), jnp.int32),
            pltpu.VMEM(own.shape, own.dtype),
            pltpu.VMEM(moveouts.shape, moveouts.dtype),
            pltpu.VMEM((1, kcount), jnp.int32),
            pltpu.VMEM((stations, taps, 2 * LANES), jnp.bfloat16),
            pltpu.SemaphoreType.DMA((5,)),
        ],
        compiler_params=pltpu.CompilerParams(vmem_limit_bytes=32 << 20),
        name="near",
    )(*(
        pltpu.with_memory_space_constraint(operand, pltpu.HBM)
        for operand in (live_mask.reshape(1, stations), own, templates, moveouts, owner_order.reshape(1, kcount))
    ))


def stack_part(ahead, near, groups):
    components, stations, block = ahead.shape
    kcount, taps = near[0].shape[1:]
    vmem = pl.BlockSpec(memory_space=pltpu.VMEM)
    return pl.pallas_call(
        stack_kernel,
        out_shape=jax.ShapeDtypeStruct((groups, kcount // groups, block), jnp.bfloat16),
        in_specs=[vmem] * (1 + len(near)),
        out_specs=vmem,
        scratch_shapes=[pltpu.VMEM((stations, taps, block), jnp.bfloat16)],
        compiler_params=pltpu.CompilerParams(vmem_limit_bytes=32 << 20),
        name="stack",
    )(ahead, *near)


def shards(record, templates, moveouts, live_mask, owner_order):
    stations, components = record.shape[:2]
    count = lax.axis_size("tm")
    groups = lax.axis_size("sta")
    own = jnp.transpose(record, (1, 0, 2))
    ahead = lax.ppermute(own, "tm", [(source, source - 1) for source in range(1, count)])
    gain = math.sqrt(components * TLEN / (stations * groups))
    near = near_part(own, templates, moveouts, live_mask, owner_order, gain)
    partial = stack_part(ahead, near, groups)
    parts = lax.all_to_all(partial, "sta", 0, 0)
    return jnp.sum(parts.astype(jnp.float32), axis=0)


def solution(mesh):
    placed = (P("sta", None, "tm"), P("sta", None, None), P("sta", None), P("sta"), P())
    return jax.shard_map(
        shards, mesh=mesh, in_specs=placed, out_specs=P("sta", "tm"), check_vma=False
    )
```

```python
import math

import jax
import jax.numpy as jnp
from jax import lax
from jax.experimental import pallas as pl
from jax.experimental.pallas import tpu as pltpu
from jax.sharding import PartitionSpec as P
TLEN = 256
MAXM = 256
LANES = 128
SPAN = 16
epsilon = 1e-05


def column_of(row, size):
    here = lax.broadcasted_iota(jnp.int32, (size, size), 0)
    there = lax.broadcasted_iota(jnp.int32, (size, size), 1)
    return jnp.sum(jnp.where(here == there, row, jnp.zeros_like(row)), axis=1, keepdims=True)


def block_of(array, i):
    return array[:, i * LANES : (i + 1) * LANES]


def backwards(ref, blocks):
    components, stations = ref.shape[:2]
    rows = jnp.concatenate([ref[c].astype(jnp.float32) for c in range(components)], axis=0)
    rows = jnp.concatenate([rows, jnp.zeros((-rows.shape[0] % 8, rows.shape[1]), jnp.float32)], axis=0)
    mirror = LANES - 1 - lax.broadcasted_iota(jnp.int32, (rows.shape[0], LANES), 1)
    return [jnp.take_along_axis(block_of(rows, i), mirror, axis=1) for i in reversed(blocks)]


def staircase(row, count, step):
    return pltpu.roll(jnp.broadcast_to(row, (count, row.shape[1])), 0, 1, stride=step, stride_axis=0)


def record_scale_of(rows, stations, s, taps):
    squares = sum(jnp.square(rows[r : r + 1]) for r in range(s, taps // TLEN * stations, stations))
    energy = jnp.sum(staircase(squares, SPAN, 1), axis=0, keepdims=True)
    energy = jnp.sum(staircase(energy, LANES // SPAN, SPAN), axis=0, keepdims=True)
    energy = energy + pltpu.roll(energy, LANES, 1)
    return 1.0 / (taps * jnp.sqrt(energy / taps + epsilon))


def lag(moveout):
    return lax.broadcasted_iota(jnp.int32, moveout.shape, 1) + (moveout & (LANES - 1))


def turn(correlation, record_scale, template_scale, reach):
    score = (correlation * record_scale * template_scale).astype(jnp.bfloat16).astype(jnp.float32)
    return jnp.take_along_axis(score, LANES - 1 - (reach & (LANES - 1)), axis=1)


def near_kernel(
    live_hbm, own_hbm, template_hbm, moveout_hbm, order_hbm,
    placed_ref, tail_ref, factor_ref, scale_ref, delay_ref, corner_ref, joined_ref, turned_ref,
    template_ref, live_ref, own_ref, moveout_ref, order_ref, frames_ref, sems, *, gain
):
    components, stations, block = own_ref.shape
    kcount, taps = template_ref.shape[1:]
    pairs = [
        (own_hbm, own_ref), (moveout_hbm, moveout_ref), (order_hbm, order_ref), (live_hbm, live_ref),
        (template_hbm, template_ref),
    ]
    copies = [pltpu.make_async_copy(*pair, sems.at[i]) for i, pair in enumerate(pairs)]
    for copy in copies[:1] + copies[2:3] + copies[-1:] + copies[1:2] + copies[3:4]:
        copy.start()
    copies[0].wait()
    copies[2].wait()
    blocks = backwards(own_ref, range(block // LANES))
    rows = jnp.concatenate(blocks, axis=1)
    last = block // LANES - 1
    for i in range(2):
        tail_ref[:, i * LANES : (i + 1) * LANES] = blocks[i]
    for s in range(stations):
        for c in range(components):
            r = c * stations + s
            steps = staircase(rows[r : r + 1], LANES, 1).astype(jnp.bfloat16)
            corner_ref[s, c * LANES : (c + 1) * LANES, :] = block_of(steps, last - 2)
            for h in range(TLEN // LANES):
                start = c * TLEN + h * LANES
                frames_ref[s, start : start + LANES, :] = steps[:, (last - 1 - h) * LANES : (last + 1 - h) * LANES]
    order = column_of(order_ref[...], kcount)
    chosen = (order == lax.broadcasted_iota(jnp.int32, (kcount, kcount), 1)).astype(jnp.bfloat16)
    for copy in (copies[1], copies[3], copies[4]):
        copy.wait()
    delays = lax.dot_general(
        chosen, moveout_ref[...].astype(jnp.bfloat16), (((1,), (1,)), ((), ())), preferred_element_type=jnp.float32
    ).astype(jnp.int32)
    for s in range(stations):
        delay_ref[s] = jnp.broadcast_to(delays[:, s : s + 1], (kcount, LANES))
        factor_ref[s] = jnp.broadcast_to(live_ref[0:1, s : s + 1].astype(jnp.float32) * gain, (8, LANES))
    for s in range(stations):
        record_scale = record_scale_of(rows, stations, s, taps)
        wide = jnp.dot(chosen, template_ref[s], preferred_element_type=jnp.float32)
        placed_ref[s] = wide.astype(jnp.bfloat16)
        energy = jnp.sum(wide * wide, axis=1, keepdims=True)
        scale = jnp.broadcast_to(1.0 / jnp.sqrt(energy / taps + epsilon), (kcount, LANES))
        scale_ref[s] = scale
        correlation = jnp.dot(placed_ref[s], frames_ref[s], preferred_element_type=jnp.float32)
        reach = lag(delay_ref[s])
        first = turn(block_of(correlation, 1), block_of(record_scale, last), scale, reach)
        second = turn(block_of(correlation, 0), block_of(record_scale, last - 1), scale, reach)
        joined_ref[s] = jnp.where(reach < LANES, first, second)
        turned_ref[s] = second


def stack_kernel(
    next_ref, placed_ref, tail_ref, factor_ref, scale_ref, delay_ref, corner_ref, joined_ref, turned_ref,
    out_ref, frames_ref
):
    components, stations, block = next_ref.shape
    kcount, taps = placed_ref.shape[1:]
    count = block // LANES
    inside = (lax.axis_index("tm") < lax.axis_size("tm") - 1).astype(jnp.float32)
    rows = jnp.concatenate([part * inside for part in backwards(next_ref, range(count))] + [tail_ref[...]], axis=1)
    total = [jnp.zeros((kcount, LANES), jnp.float32) for _ in range(count)]
    for s in range(stations):
        for c in range(components):
            r = c * stations + s
            steps = staircase(rows[r : r + 1, : (count + 1) * LANES], LANES, 1).astype(jnp.bfloat16)
            start = c * TLEN
            frames_ref[s, start : start + LANES, : (count - 1) * LANES] = steps[:, 2 * LANES :]
            frames_ref[s, start : start + LANES, (count - 1) * LANES :] = corner_ref[s, c * LANES : (c + 1) * LANES, :]
            frames_ref[s, start + LANES : start + TLEN, :] = steps[:, LANES:]
    for s in range(stations):
        record_scale = record_scale_of(rows, stations, s, taps)
        correlation = jnp.dot(placed_ref[s], frames_ref[s], preferred_element_type=jnp.float32)
        moveout = delay_ref[s]
        reach = lag(moveout)
        far = moveout >= LANES
        factor = factor_ref[s, 0:1]
        turned = [turned_ref[s]] + [
            turn(block_of(correlation, i), block_of(record_scale, 2 + i), scale_ref[s], reach)
            for i in reversed(range(count))
        ]
        joined = [joined_ref[s]] + [jnp.where(reach < LANES, turned[i], turned[i + 1]) for i in range(count)]
        for i in range(count):
            total[i] = total[i] + jnp.where(far, joined[i + 1], joined[i]) * factor
    out_ref[...] = jnp.concatenate(total, axis=1).astype(jnp.bfloat16).reshape(out_ref.shape)


def near_part(own, templates, moveouts, live_mask, owner_order, gain):
    components, stations, block = own.shape
    kcount, taps = templates.shape[1:]
    row = (stations, kcount, LANES)
    shapes = [
        (templates.shape, jnp.bfloat16), ((-(-components * stations // 8) * 8, 2 * LANES), jnp.float32),
        ((stations, 8, LANES), jnp.float32), (row, jnp.float32), (row, jnp.int32),
        ((stations, taps // 2, LANES), jnp.bfloat16), (row, jnp.float32), (row, jnp.float32),
    ]
    return pl.pallas_call(
        lambda *refs: near_kernel(*refs, gain=gain),
        out_shape=[jax.ShapeDtypeStruct(*shape) for shape in shapes],
        in_specs=[pl.BlockSpec(memory_space=pltpu.HBM)] * 5,
        out_specs=[pl.BlockSpec(memory_space=pltpu.VMEM)] * len(shapes),
        scratch_shapes=[
            pltpu.VMEM(templates.shape, templates.dtype),
            pltpu.VMEM((1, stations), jnp.int32),
            pltpu.VMEM(own.shape, own.dtype),
            pltpu.VMEM(moveouts.shape, moveouts.dtype),
            pltpu.VMEM((1, kcount), jnp.int32),
            pltpu.VMEM((stations, taps, 2 * LANES), jnp.bfloat16),
            pltpu.SemaphoreType.DMA((5,)),
        ],
        compiler_params=pltpu.CompilerParams(vmem_limit_bytes=32 << 20),
        name="near",
    )(*(
        pltpu.with_memory_space_constraint(operand, pltpu.HBM)
        for operand in (live_mask.reshape(1, stations), own, templates, moveouts, owner_order.reshape(1, kcount))
    ))


def stack_part(ahead, near, groups):
    components, stations, block = ahead.shape
    kcount, taps = near[0].shape[1:]
    vmem = pl.BlockSpec(memory_space=pltpu.VMEM)
    return pl.pallas_call(
        stack_kernel,
        out_shape=jax.ShapeDtypeStruct((groups, kcount // groups, block), jnp.bfloat16),
        in_specs=[vmem] * (1 + len(near)),
        out_specs=vmem,
        scratch_shapes=[pltpu.VMEM((stations, taps, block), jnp.bfloat16)],
        compiler_params=pltpu.CompilerParams(vmem_limit_bytes=32 << 20),
        name="stack",
    )(ahead, *near)


def shards(record, templates, moveouts, live_mask, owner_order):
    stations, components = record.shape[:2]
    count = lax.axis_size("tm")
    groups = lax.axis_size("sta")
    own = jnp.transpose(record, (1, 0, 2))
    ahead = lax.ppermute(own, "tm", [(source, (source - 1) % count) for source in range(count)])
    gain = math.sqrt(components * TLEN / (stations * groups))
    near = near_part(own, templates, moveouts, live_mask, owner_order, gain)
    partial = stack_part(ahead, near, groups)
    parts = lax.all_to_all(partial, "sta", 0, 0)
    return jnp.sum(parts.astype(jnp.float32), axis=0)


def solution(mesh):
    placed = (P("sta", None, "tm"), P("sta", None, None), P("sta", None), P("sta"), P())
    return jax.shard_map(
        shards, mesh=mesh, in_specs=placed, out_specs=P("sta", "tm"), check_vma=False
    )
```

```python
import math

import jax
import jax.numpy as jnp
from jax import lax
from jax.experimental import pallas as pl
from jax.experimental.pallas import tpu as pltpu
from jax.sharding import PartitionSpec as P
TLEN = 256
MAXM = 256
LANES = 128
SPAN = 16
epsilon = 1e-05


def column_of(row, size):
    here = lax.broadcasted_iota(jnp.int32, (size, size), 0)
    there = lax.broadcasted_iota(jnp.int32, (size, size), 1)
    return jnp.sum(jnp.where(here == there, row, jnp.zeros_like(row)), axis=1, keepdims=True)


def block_of(array, i):
    return array[:, i * LANES : (i + 1) * LANES]


def backwards(ref, blocks):
    components, stations = ref.shape[:2]
    rows = jnp.concatenate([ref[c].astype(jnp.float32) for c in range(components)], axis=0)
    rows = jnp.concatenate([rows, jnp.zeros((-rows.shape[0] % 8, rows.shape[1]), jnp.float32)], axis=0)
    mirror = LANES - 1 - lax.broadcasted_iota(jnp.int32, (rows.shape[0], LANES), 1)
    return [jnp.take_along_axis(block_of(rows, i), mirror, axis=1) for i in reversed(blocks)]


def staircase(row, count, step):
    return pltpu.roll(jnp.broadcast_to(row, (count, row.shape[1])), 0, 1, stride=step, stride_axis=0)


def record_scale_of(rows, stations, s, taps):
    squares = sum(jnp.square(rows[r : r + 1]) for r in range(s, taps // TLEN * stations, stations))
    energy = jnp.sum(staircase(squares, SPAN, 1), axis=0, keepdims=True)
    energy = jnp.sum(staircase(energy, LANES // SPAN, SPAN), axis=0, keepdims=True)
    energy = energy + pltpu.roll(energy, LANES, 1)
    return 1.0 / (taps * jnp.sqrt(energy / taps + epsilon))


def lag(moveout):
    return lax.broadcasted_iota(jnp.int32, moveout.shape, 1) + (moveout & (LANES - 1))


def turn(correlation, record_scale, template_scale, reach):
    score = (correlation * record_scale * template_scale).astype(jnp.bfloat16).astype(jnp.float32)
    return jnp.take_along_axis(score, LANES - 1 - (reach & (LANES - 1)), axis=1)


def near_kernel(
    live_hbm, own_hbm, template_hbm, moveout_hbm, order_hbm,
    placed_ref, tail_ref, factor_ref, scale_ref, delay_ref, corner_ref, joined_ref, turned_ref,
    template_ref, live_ref, own_ref, moveout_ref, order_ref, frames_ref, sems, *, gain
):
    components, stations, block = own_ref.shape
    kcount, taps = template_ref.shape[1:]
    pairs = [
        (own_hbm, own_ref), (moveout_hbm, moveout_ref), (order_hbm, order_ref), (live_hbm, live_ref),
        (template_hbm, template_ref),
    ]
    copies = [pltpu.make_async_copy(*pair, sems.at[i]) for i, pair in enumerate(pairs)]
    for copy in copies[:1] + copies[2:3] + copies[-1:] + copies[1:2] + copies[3:4]:
        copy.start()
    copies[0].wait()
    copies[2].wait()
    blocks = backwards(own_ref, range(block // LANES))
    rows = jnp.concatenate(blocks, axis=1)
    last = block // LANES - 1
    for i in range(2):
        tail_ref[:, i * LANES : (i + 1) * LANES] = blocks[i]
    for s in range(stations):
        for c in range(components):
            r = c * stations + s
            steps = staircase(rows[r : r + 1], LANES, 1).astype(jnp.bfloat16)
            corner_ref[s, c * LANES : (c + 1) * LANES, :] = block_of(steps, last - 2)
            for h in range(TLEN // LANES):
                start = c * TLEN + h * LANES
                frames_ref[s, start : start + LANES, :] = steps[:, (last - 1 - h) * LANES : (last + 1 - h) * LANES]
    order = column_of(order_ref[...], kcount)
    chosen = (order == lax.broadcasted_iota(jnp.int32, (kcount, kcount), 1)).astype(jnp.bfloat16)
    for copy in (copies[1], copies[3], copies[4]):
        copy.wait()
    delays = lax.dot_general(
        chosen, moveout_ref[...].astype(jnp.bfloat16), (((1,), (1,)), ((), ())), preferred_element_type=jnp.float32
    ).astype(jnp.int32)
    for s in range(stations):
        delay_ref[s] = jnp.broadcast_to(delays[:, s : s + 1], (kcount, LANES))
        factor_ref[s] = jnp.broadcast_to(live_ref[0:1, s : s + 1].astype(jnp.float32) * gain, (8, LANES))
    for s in range(stations):
        record_scale = record_scale_of(rows, stations, s, taps)
        wide = jnp.dot(chosen, template_ref[s], preferred_element_type=jnp.float32)
        placed_ref[s] = wide.astype(jnp.bfloat16)
        energy = jnp.sum(wide * wide, axis=1, keepdims=True)
        scale = jnp.broadcast_to(1.0 / jnp.sqrt(energy / taps + epsilon), (kcount, LANES))
        scale_ref[s] = scale
        correlation = jnp.dot(placed_ref[s], frames_ref[s], preferred_element_type=jnp.float32)
        reach = lag(delay_ref[s])
        first = turn(block_of(correlation, 1), block_of(record_scale, last), scale, reach)
        second = turn(block_of(correlation, 0), block_of(record_scale, last - 1), scale, reach)
        joined_ref[s] = jnp.where(reach < LANES, first, second)
        turned_ref[s] = second


def stack_kernel(
    chip_ref, next_ref, placed_ref, tail_ref, factor_ref, scale_ref, delay_ref, corner_ref, joined_ref, turned_ref,
    out_ref, frames_ref
):
    components, stations, block = next_ref.shape
    kcount, taps = placed_ref.shape[1:]
    count = block // LANES
    place = lax.axis_index("tm")
    even = (place % 2 == 0).astype(jnp.float32)
    odd = (1.0 - even) * (place < lax.axis_size("tm") - 1).astype(jnp.float32)
    arrived = zip(backwards(chip_ref, range(count)), backwards(next_ref, range(count)))
    rows = jnp.concatenate([near * even + far * odd for near, far in arrived] + [tail_ref[...]], axis=1)
    total = [jnp.zeros((kcount, LANES), jnp.float32) for _ in range(count)]
    for s in range(stations):
        for c in range(components):
            r = c * stations + s
            steps = staircase(rows[r : r + 1, : (count + 1) * LANES], LANES, 1).astype(jnp.bfloat16)
            start = c * TLEN
            frames_ref[s, start : start + LANES, : (count - 1) * LANES] = steps[:, 2 * LANES :]
            frames_ref[s, start : start + LANES, (count - 1) * LANES :] = corner_ref[s, c * LANES : (c + 1) * LANES, :]
            frames_ref[s, start + LANES : start + TLEN, :] = steps[:, LANES:]
    for s in range(stations):
        record_scale = record_scale_of(rows, stations, s, taps)
        correlation = jnp.dot(placed_ref[s], frames_ref[s], preferred_element_type=jnp.float32)
        moveout = delay_ref[s]
        reach = lag(moveout)
        far = moveout >= LANES
        factor = factor_ref[s, 0:1]
        turned = [turned_ref[s]] + [
            turn(block_of(correlation, i), block_of(record_scale, 2 + i), scale_ref[s], reach)
            for i in reversed(range(count))
        ]
        joined = [joined_ref[s]] + [jnp.where(reach < LANES, turned[i], turned[i + 1]) for i in range(count)]
        for i in range(count):
            total[i] = total[i] + jnp.where(far, joined[i + 1], joined[i]) * factor
    out_ref[...] = jnp.concatenate(total, axis=1).astype(jnp.bfloat16).reshape(out_ref.shape)


def near_part(own, templates, moveouts, live_mask, owner_order, gain):
    components, stations, block = own.shape
    kcount, taps = templates.shape[1:]
    row = (stations, kcount, LANES)
    shapes = [
        (templates.shape, jnp.bfloat16), ((-(-components * stations // 8) * 8, 2 * LANES), jnp.float32),
        ((stations, 8, LANES), jnp.float32), (row, jnp.float32), (row, jnp.int32),
        ((stations, taps // 2, LANES), jnp.bfloat16), (row, jnp.float32), (row, jnp.float32),
    ]
    return pl.pallas_call(
        lambda *refs: near_kernel(*refs, gain=gain),
        out_shape=[jax.ShapeDtypeStruct(*shape) for shape in shapes],
        in_specs=[pl.BlockSpec(memory_space=pltpu.HBM)] * 5,
        out_specs=[pl.BlockSpec(memory_space=pltpu.VMEM)] * len(shapes),
        scratch_shapes=[
            pltpu.VMEM(templates.shape, templates.dtype),
            pltpu.VMEM((1, stations), jnp.int32),
            pltpu.VMEM(own.shape, own.dtype),
            pltpu.VMEM(moveouts.shape, moveouts.dtype),
            pltpu.VMEM((1, kcount), jnp.int32),
            pltpu.VMEM((stations, taps, 2 * LANES), jnp.bfloat16),
            pltpu.SemaphoreType.DMA((5,)),
        ],
        compiler_params=pltpu.CompilerParams(vmem_limit_bytes=32 << 20),
        name="near",
    )(*(
        pltpu.with_memory_space_constraint(operand, pltpu.HBM)
        for operand in (live_mask.reshape(1, stations), own, templates, moveouts, owner_order.reshape(1, kcount))
    ))


def stack_part(ahead, near, groups):
    components, stations, block = ahead[0].shape
    kcount, taps = near[0].shape[1:]
    vmem = pl.BlockSpec(memory_space=pltpu.VMEM)
    return pl.pallas_call(
        stack_kernel,
        out_shape=jax.ShapeDtypeStruct((groups, kcount // groups, block), jnp.bfloat16),
        in_specs=[vmem] * (len(ahead) + len(near)),
        out_specs=vmem,
        scratch_shapes=[pltpu.VMEM((stations, taps, block), jnp.bfloat16)],
        compiler_params=pltpu.CompilerParams(vmem_limit_bytes=32 << 20),
        name="stack",
    )(*ahead, *near)


def swaps(count, first):
    pairs = [(i, i) for i in range(count)]
    for i in range(first, count - 1, 2):
        pairs[i], pairs[i + 1] = (i, i + 1), (i + 1, i)
    return pairs


def shards(record, templates, moveouts, live_mask, owner_order):
    stations, components = record.shape[:2]
    count = lax.axis_size("tm")
    groups = lax.axis_size("sta")
    own = jnp.transpose(record, (1, 0, 2))
    ahead = (lax.ppermute(own, "tm", swaps(count, 0)), lax.ppermute(own, "tm", swaps(count, 1)))
    gain = math.sqrt(components * TLEN / (stations * groups))
    near = near_part(own, templates, moveouts, live_mask, owner_order, gain)
    partial = stack_part(ahead, near, groups)
    parts = lax.all_to_all(partial, "sta", 0, 0)
    return jnp.sum(parts.astype(jnp.float32), axis=0)


def solution(mesh):
    placed = (P("sta", None, "tm"), P("sta", None, None), P("sta", None), P("sta"), P())
    return jax.shard_map(
        shards, mesh=mesh, in_specs=placed, out_specs=P("sta", "tm"), check_vma=False
    )
```

```python
import math

import jax
import jax.numpy as jnp
from jax import lax
from jax.experimental import pallas as pl
from jax.experimental.pallas import tpu as pltpu
from jax.sharding import PartitionSpec as P
TLEN = 256
MAXM = 256
LANES = 128
SPAN = 16
epsilon = 1e-05


def column_of(row, size):
    here = lax.broadcasted_iota(jnp.int32, (size, size), 0)
    there = lax.broadcasted_iota(jnp.int32, (size, size), 1)
    return jnp.sum(jnp.where(here == there, row, jnp.zeros_like(row)), axis=1, keepdims=True)


def block_of(array, i):
    return array[:, i * LANES : (i + 1) * LANES]


def backwards(ref, blocks):
    components, stations = ref.shape[:2]
    rows = jnp.concatenate([ref[c].astype(jnp.float32) for c in range(components)], axis=0)
    rows = jnp.concatenate([rows, jnp.zeros((-rows.shape[0] % 8, rows.shape[1]), jnp.float32)], axis=0)
    mirror = LANES - 1 - lax.broadcasted_iota(jnp.int32, (rows.shape[0], LANES), 1)
    return [jnp.take_along_axis(block_of(rows, i), mirror, axis=1) for i in reversed(blocks)]


def staircase(row, count, step):
    return pltpu.roll(jnp.broadcast_to(row, (count, row.shape[1])), 0, 1, stride=step, stride_axis=0)


def record_scale_of(rows, stations, s, taps):
    squares = sum(jnp.square(rows[r : r + 1]) for r in range(s, taps // TLEN * stations, stations))
    energy = jnp.sum(staircase(squares, SPAN, 1), axis=0, keepdims=True)
    energy = jnp.sum(staircase(energy, LANES // SPAN, SPAN), axis=0, keepdims=True)
    energy = energy + pltpu.roll(energy, LANES, 1)
    return 1.0 / (taps * jnp.sqrt(energy / taps + epsilon))


def lag(moveout):
    return lax.broadcasted_iota(jnp.int32, moveout.shape, 1) + (moveout & (LANES - 1))


def turn(correlation, record_scale, template_scale, reach):
    score = (correlation * record_scale * template_scale).astype(jnp.bfloat16).astype(jnp.float32)
    return jnp.take_along_axis(score, LANES - 1 - (reach & (LANES - 1)), axis=1)


def near_kernel(
    live_hbm, own_hbm, template_hbm, moveout_hbm, order_hbm,
    placed_ref, tail_ref, factor_ref, scale_ref, delay_ref, corner_ref, joined_ref, turned_ref,
    template_ref, live_ref, own_ref, moveout_ref, order_ref, frames_ref, sems, *, gain
):
    components, stations, block = own_ref.shape
    kcount, taps = template_ref.shape[1:]
    pairs = [
        (own_hbm, own_ref), (moveout_hbm, moveout_ref), (order_hbm, order_ref), (live_hbm, live_ref),
        (template_hbm, template_ref),
    ]
    copies = [pltpu.make_async_copy(*pair, sems.at[i]) for i, pair in enumerate(pairs)]
    for copy in copies[:1] + copies[2:3] + copies[-1:] + copies[1:2] + copies[3:4]:
        copy.start()
    copies[0].wait()
    copies[2].wait()
    blocks = backwards(own_ref, range(block // LANES))
    rows = jnp.concatenate(blocks, axis=1)
    last = block // LANES - 1
    for i in range(2):
        tail_ref[:, i * LANES : (i + 1) * LANES] = blocks[i]
    for s in range(stations):
        for c in range(components):
            r = c * stations + s
            steps = staircase(rows[r : r + 1], LANES, 1).astype(jnp.bfloat16)
            corner_ref[s, c * LANES : (c + 1) * LANES, :] = block_of(steps, last - 2)
            for h in range(TLEN // LANES):
                start = c * TLEN + h * LANES
                frames_ref[s, start : start + LANES, :] = steps[:, (last - 1 - h) * LANES : (last + 1 - h) * LANES]
    order = column_of(order_ref[...], kcount)
    chosen = (order == lax.broadcasted_iota(jnp.int32, (kcount, kcount), 1)).astype(jnp.bfloat16)
    for copy in (copies[1], copies[3], copies[4]):
        copy.wait()
    delays = lax.dot_general(
        chosen, moveout_ref[...].astype(jnp.bfloat16), (((1,), (1,)), ((), ())), preferred_element_type=jnp.float32
    ).astype(jnp.int32)
    for s in range(stations):
        delay_ref[s] = jnp.broadcast_to(delays[:, s : s + 1], (kcount, LANES))
        factor_ref[s] = jnp.broadcast_to(live_ref[0:1, s : s + 1].astype(jnp.float32) * gain, (8, LANES))
    for s in range(stations):
        record_scale = record_scale_of(rows, stations, s, taps)
        wide = jnp.dot(chosen, template_ref[s], preferred_element_type=jnp.float32)
        placed_ref[s] = wide.astype(jnp.bfloat16)
        energy = jnp.sum(wide * wide, axis=1, keepdims=True)
        scale = jnp.broadcast_to(1.0 / jnp.sqrt(energy / taps + epsilon), (kcount, LANES))
        scale_ref[s] = scale
        correlation = jnp.dot(placed_ref[s], frames_ref[s], preferred_element_type=jnp.float32)
        reach = lag(delay_ref[s])
        first = turn(block_of(correlation, 1), block_of(record_scale, last), scale, reach)
        second = turn(block_of(correlation, 0), block_of(record_scale, last - 1), scale, reach)
        joined_ref[s] = jnp.where(reach < LANES, first, second)
        turned_ref[s] = second


def stack_kernel(
    chip_ref, next_ref, placed_ref, tail_ref, factor_ref, scale_ref, delay_ref, corner_ref, joined_ref, turned_ref,
    out_ref, frames_ref
):
    components, stations, block = next_ref.shape
    kcount, taps = placed_ref.shape[1:]
    count = block // LANES
    place = lax.axis_index("tm")
    even = (place % 2 == 0).astype(jnp.float32)
    odd = (1.0 - even) * (place < lax.axis_size("tm") - 1).astype(jnp.float32)
    arrived = zip(backwards(chip_ref, range(count)), backwards(next_ref, range(count)))
    rows = jnp.concatenate([near * even + far * odd for near, far in arrived] + [tail_ref[...]], axis=1)
    total = [jnp.zeros((kcount, LANES), jnp.float32) for _ in range(count)]
    for s in range(stations):
        for c in range(components):
            r = c * stations + s
            steps = staircase(rows[r : r + 1, : (count + 1) * LANES], LANES, 1).astype(jnp.bfloat16)
            start = c * TLEN
            frames_ref[s, start : start + LANES, : (count - 1) * LANES] = steps[:, 2 * LANES :]
            frames_ref[s, start : start + LANES, (count - 1) * LANES :] = corner_ref[s, c * LANES : (c + 1) * LANES, :]
            frames_ref[s, start + LANES : start + TLEN, :] = steps[:, LANES:]
    for s in range(stations):
        record_scale = record_scale_of(rows, stations, s, taps)
        correlation = jnp.dot(placed_ref[s], frames_ref[s], preferred_element_type=jnp.float32)
        moveout = delay_ref[s]
        reach = lag(moveout)
        far = moveout >= LANES
        factor = factor_ref[s, 0:1]
        turned = [turned_ref[s]] + [
            turn(block_of(correlation, i), block_of(record_scale, 2 + i), scale_ref[s], reach)
            for i in reversed(range(count))
        ]
        joined = [joined_ref[s]] + [jnp.where(reach < LANES, turned[i], turned[i + 1]) for i in range(count)]
        for i in range(count):
            total[i] = total[i] + jnp.where(far, joined[i + 1], joined[i]) * factor
    out_ref[...] = jnp.concatenate(total, axis=1).astype(jnp.bfloat16).reshape(out_ref.shape)


def near_part(own, templates, moveouts, live_mask, owner_order, gain):
    components, stations, block = own.shape
    kcount, taps = templates.shape[1:]
    row = (stations, kcount, LANES)
    shapes = [
        (templates.shape, jnp.bfloat16), ((-(-components * stations // 8) * 8, 2 * LANES), jnp.float32),
        ((stations, 8, LANES), jnp.float32), (row, jnp.float32), (row, jnp.int32),
        ((stations, taps // 2, LANES), jnp.bfloat16), (row, jnp.float32), (row, jnp.float32),
    ]
    return pl.pallas_call(
        lambda *refs: near_kernel(*refs, gain=gain),
        out_shape=[jax.ShapeDtypeStruct(*shape) for shape in shapes],
        in_specs=[pl.BlockSpec(memory_space=pltpu.HBM)] * 5,
        out_specs=[pl.BlockSpec(memory_space=pltpu.VMEM)] * len(shapes),
        scratch_shapes=[
            pltpu.VMEM(templates.shape, templates.dtype),
            pltpu.VMEM((1, stations), jnp.int32),
            pltpu.VMEM(own.shape, own.dtype),
            pltpu.VMEM(moveouts.shape, moveouts.dtype),
            pltpu.VMEM((1, kcount), jnp.int32),
            pltpu.VMEM((stations, taps, 2 * LANES), jnp.bfloat16),
            pltpu.SemaphoreType.DMA((5,)),
        ],
        compiler_params=pltpu.CompilerParams(vmem_limit_bytes=32 << 20),
        name="near",
    )(*(
        pltpu.with_memory_space_constraint(operand, pltpu.HBM)
        for operand in (live_mask.reshape(1, stations), own, templates, moveouts, owner_order.reshape(1, kcount))
    ))


def stack_part(ahead, near, groups):
    components, stations, block = ahead[0].shape
    kcount, taps = near[0].shape[1:]
    vmem = pl.BlockSpec(memory_space=pltpu.VMEM)
    return pl.pallas_call(
        stack_kernel,
        out_shape=jax.ShapeDtypeStruct((groups, kcount // groups, block), jnp.bfloat16),
        in_specs=[vmem] * (len(ahead) + len(near)),
        out_specs=vmem,
        scratch_shapes=[pltpu.VMEM((stations, taps, block), jnp.bfloat16)],
        compiler_params=pltpu.CompilerParams(vmem_limit_bytes=32 << 20),
        name="stack",
    )(*ahead, *near)


def swaps(count, first):
    pairs = {}
    for i in range(first, count - 1, 2):
        pairs[i], pairs[i + 1] = i + 1, i
    if first:
        end = count - 1
        pairs.update({0: 2, 1: 0, end: end - 1, end - 2: end})
    return list(pairs.items())


def shards(record, templates, moveouts, live_mask, owner_order):
    stations, components = record.shape[:2]
    count = lax.axis_size("tm")
    groups = lax.axis_size("sta")
    own = jnp.transpose(record, (1, 0, 2))
    ahead = (lax.ppermute(own, "tm", swaps(count, 0)), lax.ppermute(own, "tm", swaps(count, 1)))
    gain = math.sqrt(components * TLEN / (stations * groups))
    near = near_part(own, templates, moveouts, live_mask, owner_order, gain)
    partial = stack_part(ahead, near, groups)
    parts = lax.all_to_all(partial, "sta", 0, 0)
    return jnp.sum(parts.astype(jnp.float32), axis=0)


def solution(mesh):
    placed = (P("sta", None, "tm"), P("sta", None, None), P("sta", None), P("sta"), P())
    return jax.shard_map(
        shards, mesh=mesh, in_specs=placed, out_specs=P("sta", "tm"), check_vma=False
    )
```

```python
import math

import jax
import jax.numpy as jnp
from jax import lax
from jax.experimental import pallas as pl
from jax.experimental.pallas import tpu as pltpu
from jax.sharding import PartitionSpec as P
TLEN = 256
MAXM = 256
LANES = 128
SPAN = 16
epsilon = 1e-05


def column_of(row, size):
    here = lax.broadcasted_iota(jnp.int32, (size, size), 0)
    there = lax.broadcasted_iota(jnp.int32, (size, size), 1)
    return jnp.sum(jnp.where(here == there, row, jnp.zeros_like(row)), axis=1, keepdims=True)


def block_of(array, i):
    return array[:, i * LANES : (i + 1) * LANES]


def backwards(ref, blocks):
    components, stations = ref.shape[:2]
    rows = jnp.concatenate([ref[c].astype(jnp.float32) for c in range(components)], axis=0)
    rows = jnp.concatenate([rows, jnp.zeros((-rows.shape[0] % 8, rows.shape[1]), jnp.float32)], axis=0)
    mirror = LANES - 1 - lax.broadcasted_iota(jnp.int32, (rows.shape[0], LANES), 1)
    return [jnp.take_along_axis(block_of(rows, i), mirror, axis=1) for i in reversed(blocks)]


def staircase(row, count, step):
    return pltpu.roll(jnp.broadcast_to(row, (count, row.shape[1])), 0, 1, stride=step, stride_axis=0)


def record_scale_of(rows, stations, s, taps):
    squares = sum(jnp.square(rows[r : r + 1]) for r in range(s, taps // TLEN * stations, stations))
    energy = jnp.sum(staircase(squares, SPAN, 1), axis=0, keepdims=True)
    energy = jnp.sum(staircase(energy, LANES // SPAN, SPAN), axis=0, keepdims=True)
    energy = energy + pltpu.roll(energy, LANES, 1)
    return 1.0 / (taps * jnp.sqrt(energy / taps + epsilon))


def lag(moveout):
    return lax.broadcasted_iota(jnp.int32, moveout.shape, 1) + (moveout & (LANES - 1))


def turn(correlation, record_scale, template_scale, reach):
    score = (correlation * record_scale * template_scale).astype(jnp.bfloat16).astype(jnp.float32)
    return jnp.take_along_axis(score, LANES - 1 - (reach & (LANES - 1)), axis=1)


def near_kernel(
    live_hbm, own_hbm, template_hbm, moveout_hbm, order_hbm,
    placed_ref, tail_ref, factor_ref, scale_ref, delay_ref, corner_ref, joined_ref, turned_ref,
    template_ref, live_ref, own_ref, moveout_ref, order_ref, frames_ref, sems, *, gain
):
    components, stations, block = own_ref.shape
    kcount, taps = template_ref.shape[1:]
    pairs = [
        (own_hbm, own_ref), (moveout_hbm, moveout_ref), (order_hbm, order_ref), (live_hbm, live_ref),
        (template_hbm, template_ref),
    ]
    copies = [pltpu.make_async_copy(*pair, sems.at[i]) for i, pair in enumerate(pairs)]
    for copy in copies[:1] + copies[2:3] + copies[-1:] + copies[1:2] + copies[3:4]:
        copy.start()
    copies[0].wait()
    copies[2].wait()
    blocks = backwards(own_ref, range(block // LANES))
    rows = jnp.concatenate(blocks, axis=1)
    last = block // LANES - 1
    for i in range(2):
        tail_ref[:, i * LANES : (i + 1) * LANES] = blocks[i]
    for s in range(stations):
        for c in range(components):
            r = c * stations + s
            steps = staircase(rows[r : r + 1], LANES, 1).astype(jnp.bfloat16)
            corner_ref[s, c * LANES : (c + 1) * LANES, :] = block_of(steps, last - 2)
            for h in range(TLEN // LANES):
                start = c * TLEN + h * LANES
                frames_ref[s, start : start + LANES, :] = steps[:, (last - 1 - h) * LANES : (last + 1 - h) * LANES]
    order = column_of(order_ref[...], kcount)
    chosen = (order == lax.broadcasted_iota(jnp.int32, (kcount, kcount), 1)).astype(jnp.bfloat16)
    for copy in (copies[1], copies[3], copies[4]):
        copy.wait()
    delays = lax.dot_general(
        chosen, moveout_ref[...].astype(jnp.bfloat16), (((1,), (1,)), ((), ())), preferred_element_type=jnp.float32
    ).astype(jnp.int32)
    for s in range(stations):
        delay_ref[s] = jnp.broadcast_to(delays[:, s : s + 1], (kcount, LANES))
        factor_ref[s] = jnp.broadcast_to(live_ref[0:1, s : s + 1].astype(jnp.float32) * gain, (8, LANES))
    for s in range(stations):
        record_scale = record_scale_of(rows, stations, s, taps)
        wide = jnp.dot(chosen, template_ref[s], preferred_element_type=jnp.float32)
        placed_ref[s] = wide.astype(jnp.bfloat16)
        energy = jnp.sum(wide * wide, axis=1, keepdims=True)
        scale = jnp.broadcast_to(1.0 / jnp.sqrt(energy / taps + epsilon), (kcount, LANES))
        scale_ref[s] = scale
        correlation = jnp.dot(placed_ref[s], frames_ref[s], preferred_element_type=jnp.float32)
        reach = lag(delay_ref[s])
        first = turn(block_of(correlation, 1), block_of(record_scale, last), scale, reach)
        second = turn(block_of(correlation, 0), block_of(record_scale, last - 1), scale, reach)
        joined_ref[s] = jnp.where(reach < LANES, first, second)
        turned_ref[s] = second


def stack_kernel(
    chip_ref, next_ref, placed_ref, tail_ref, factor_ref, scale_ref, delay_ref, corner_ref, joined_ref, turned_ref,
    out_ref, frames_ref
):
    components, stations, block = next_ref.shape
    kcount, taps = placed_ref.shape[1:]
    count = block // LANES
    place = lax.axis_index("tm")
    near = (place % 4 == 0).astype(jnp.float32)
    far = (1.0 - near) * (place < lax.axis_size("tm") - 1).astype(jnp.float32)
    arrived = zip(backwards(chip_ref, range(count)), backwards(next_ref, range(count)))
    rows = jnp.concatenate([chip * near + other * far for chip, other in arrived] + [tail_ref[...]], axis=1)
    total = [jnp.zeros((kcount, LANES), jnp.float32) for _ in range(count)]
    for s in range(stations):
        for c in range(components):
            r = c * stations + s
            steps = staircase(rows[r : r + 1, : (count + 1) * LANES], LANES, 1).astype(jnp.bfloat16)
            start = c * TLEN
            frames_ref[s, start : start + LANES, : (count - 1) * LANES] = steps[:, 2 * LANES :]
            frames_ref[s, start : start + LANES, (count - 1) * LANES :] = corner_ref[s, c * LANES : (c + 1) * LANES, :]
            frames_ref[s, start + LANES : start + TLEN, :] = steps[:, LANES:]
    for s in range(stations):
        record_scale = record_scale_of(rows, stations, s, taps)
        correlation = jnp.dot(placed_ref[s], frames_ref[s], preferred_element_type=jnp.float32)
        moveout = delay_ref[s]
        reach = lag(moveout)
        far = moveout >= LANES
        factor = factor_ref[s, 0:1]
        turned = [turned_ref[s]] + [
            turn(block_of(correlation, i), block_of(record_scale, 2 + i), scale_ref[s], reach)
            for i in reversed(range(count))
        ]
        joined = [joined_ref[s]] + [jnp.where(reach < LANES, turned[i], turned[i + 1]) for i in range(count)]
        for i in range(count):
            total[i] = total[i] + jnp.where(far, joined[i + 1], joined[i]) * factor
    out_ref[...] = jnp.concatenate(total, axis=1).astype(jnp.bfloat16).reshape(out_ref.shape)


def near_part(own, templates, moveouts, live_mask, owner_order, gain):
    components, stations, block = own.shape
    kcount, taps = templates.shape[1:]
    row = (stations, kcount, LANES)
    shapes = [
        (templates.shape, jnp.bfloat16), ((-(-components * stations // 8) * 8, 2 * LANES), jnp.float32),
        ((stations, 8, LANES), jnp.float32), (row, jnp.float32), (row, jnp.int32),
        ((stations, taps // 2, LANES), jnp.bfloat16), (row, jnp.float32), (row, jnp.float32),
    ]
    return pl.pallas_call(
        lambda *refs: near_kernel(*refs, gain=gain),
        out_shape=[jax.ShapeDtypeStruct(*shape) for shape in shapes],
        in_specs=[pl.BlockSpec(memory_space=pltpu.HBM)] * 5,
        out_specs=[pl.BlockSpec(memory_space=pltpu.VMEM)] * len(shapes),
        scratch_shapes=[
            pltpu.VMEM(templates.shape, templates.dtype),
            pltpu.VMEM((1, stations), jnp.int32),
            pltpu.VMEM(own.shape, own.dtype),
            pltpu.VMEM(moveouts.shape, moveouts.dtype),
            pltpu.VMEM((1, kcount), jnp.int32),
            pltpu.VMEM((stations, taps, 2 * LANES), jnp.bfloat16),
            pltpu.SemaphoreType.DMA((5,)),
        ],
        compiler_params=pltpu.CompilerParams(vmem_limit_bytes=32 << 20),
        name="near",
    )(*(
        pltpu.with_memory_space_constraint(operand, pltpu.HBM)
        for operand in (live_mask.reshape(1, stations), own, templates, moveouts, owner_order.reshape(1, kcount))
    ))


def stack_part(ahead, near, groups):
    components, stations, block = ahead[0].shape
    kcount, taps = near[0].shape[1:]
    vmem = pl.BlockSpec(memory_space=pltpu.VMEM)
    return pl.pallas_call(
        stack_kernel,
        out_shape=jax.ShapeDtypeStruct((groups, kcount // groups, block), jnp.bfloat16),
        in_specs=[vmem] * (len(ahead) + len(near)),
        out_specs=vmem,
        scratch_shapes=[pltpu.VMEM((stations, taps, block), jnp.bfloat16)],
        compiler_params=pltpu.CompilerParams(vmem_limit_bytes=32 << 20),
        name="stack",
    )(*ahead, *near)


def swapped(count):
    return [(i, i ^ 1) for i in range(count)]


def backward(count):
    pairs = {i: i - 1 for i in range(1, count)}
    pairs.update({i: i + 3 for i in range(5, count - 3, 4)})
    pairs.update({0: 4, count - 3: count - 1})
    return list(pairs.items())


def shards(record, templates, moveouts, live_mask, owner_order):
    stations, components = record.shape[:2]
    count = lax.axis_size("tm")
    groups = lax.axis_size("sta")
    own = jnp.transpose(record, (1, 0, 2))
    ahead = (lax.ppermute(own, "tm", swapped(count)), lax.ppermute(own, "tm", backward(count)))
    gain = math.sqrt(components * TLEN / (stations * groups))
    near = near_part(own, templates, moveouts, live_mask, owner_order, gain)
    partial = stack_part(ahead, near, groups)
    parts = lax.all_to_all(partial, "sta", 0, 0)
    return jnp.sum(parts.astype(jnp.float32), axis=0)


def solution(mesh):
    placed = (P("sta", None, "tm"), P("sta", None, None), P("sta", None), P("sta"), P())
    return jax.shard_map(
        shards, mesh=mesh, in_specs=placed, out_specs=P("sta", "tm"), check_vma=False
    )
```

```python
import math

import jax
import jax.numpy as jnp
from jax import lax
from jax.experimental import pallas as pl
from jax.experimental.pallas import tpu as pltpu
from jax.sharding import PartitionSpec as P
TLEN = 256
MAXM = 256
LANES = 128
SPAN = 16
epsilon = 1e-05


def column_of(row, size):
    here = lax.broadcasted_iota(jnp.int32, (size, size), 0)
    there = lax.broadcasted_iota(jnp.int32, (size, size), 1)
    return jnp.sum(jnp.where(here == there, row, jnp.zeros_like(row)), axis=1, keepdims=True)


def block_of(array, i):
    return array[:, i * LANES : (i + 1) * LANES]


def backwards(ref, blocks):
    components, stations = ref.shape[:2]
    rows = jnp.concatenate([ref[c].astype(jnp.float32) for c in range(components)], axis=0)
    rows = jnp.concatenate([rows, jnp.zeros((-rows.shape[0] % 8, rows.shape[1]), jnp.float32)], axis=0)
    mirror = LANES - 1 - lax.broadcasted_iota(jnp.int32, (rows.shape[0], LANES), 1)
    return [jnp.take_along_axis(block_of(rows, i), mirror, axis=1) for i in reversed(blocks)]


def staircase(row, count, step):
    return pltpu.roll(jnp.broadcast_to(row, (count, row.shape[1])), 0, 1, stride=step, stride_axis=0)


def record_scale_of(rows, stations, s, taps):
    squares = sum(jnp.square(rows[r : r + 1]) for r in range(s, taps // TLEN * stations, stations))
    energy = jnp.sum(staircase(squares, SPAN, 1), axis=0, keepdims=True)
    energy = jnp.sum(staircase(energy, LANES // SPAN, SPAN), axis=0, keepdims=True)
    energy = energy + pltpu.roll(energy, LANES, 1)
    return 1.0 / (taps * jnp.sqrt(energy / taps + epsilon))


def lag(moveout):
    return lax.broadcasted_iota(jnp.int32, moveout.shape, 1) + (moveout & (LANES - 1))


def turn(correlation, record_scale, template_scale, reach):
    score = (correlation * record_scale * template_scale).astype(jnp.bfloat16).astype(jnp.float32)
    return jnp.take_along_axis(score, LANES - 1 - (reach & (LANES - 1)), axis=1)


def near_kernel(
    live_hbm, own_hbm, template_hbm, moveout_hbm, order_hbm,
    placed_ref, tail_ref, factor_ref, scale_ref, delay_ref, corner_ref, joined_ref, turned_ref,
    template_ref, live_ref, own_ref, moveout_ref, order_ref, frames_ref, sems, *, gain
):
    components, stations, block = own_ref.shape
    kcount, taps = template_ref.shape[1:]
    pairs = [
        (own_hbm, own_ref), (moveout_hbm, moveout_ref), (order_hbm, order_ref), (live_hbm, live_ref),
        (template_hbm, template_ref),
    ]
    copies = [pltpu.make_async_copy(*pair, sems.at[i]) for i, pair in enumerate(pairs)]
    for copy in copies[:1] + copies[2:3] + copies[-1:] + copies[1:2] + copies[3:4]:
        copy.start()
    copies[0].wait()
    copies[2].wait()
    blocks = backwards(own_ref, range(block // LANES))
    rows = jnp.concatenate(blocks, axis=1)
    last = block // LANES - 1
    for i in range(2):
        tail_ref[:, i * LANES : (i + 1) * LANES] = blocks[i]
    for s in range(stations):
        for c in range(components):
            r = c * stations + s
            steps = staircase(rows[r : r + 1], LANES, 1).astype(jnp.bfloat16)
            corner_ref[s, c * LANES : (c + 1) * LANES, :] = block_of(steps, last - 2)
            for h in range(TLEN // LANES):
                start = c * TLEN + h * LANES
                frames_ref[s, start : start + LANES, :] = steps[:, (last - 1 - h) * LANES : (last + 1 - h) * LANES]
    order = column_of(order_ref[...], kcount)
    chosen = (order == lax.broadcasted_iota(jnp.int32, (kcount, kcount), 1)).astype(jnp.bfloat16)
    for copy in (copies[1], copies[3], copies[4]):
        copy.wait()
    delays = lax.dot_general(
        chosen, moveout_ref[...].astype(jnp.bfloat16), (((1,), (1,)), ((), ())), preferred_element_type=jnp.float32
    ).astype(jnp.int32)
    for s in range(stations):
        delay_ref[s] = jnp.broadcast_to(delays[:, s : s + 1], (kcount, LANES))
        factor_ref[s] = jnp.broadcast_to(live_ref[0:1, s : s + 1].astype(jnp.float32) * gain, (8, LANES))
    for s in range(stations):
        record_scale = record_scale_of(rows, stations, s, taps)
        wide = jnp.dot(chosen, template_ref[s], preferred_element_type=jnp.float32)
        placed_ref[s] = wide.astype(jnp.bfloat16)
        energy = jnp.sum(wide * wide, axis=1, keepdims=True)
        scale = jnp.broadcast_to(1.0 / jnp.sqrt(energy / taps + epsilon), (kcount, LANES))
        scale_ref[s] = scale
        correlation = jnp.dot(placed_ref[s], frames_ref[s], preferred_element_type=jnp.float32)
        reach = lag(delay_ref[s])
        first = turn(block_of(correlation, 1), block_of(record_scale, last), scale, reach)
        second = turn(block_of(correlation, 0), block_of(record_scale, last - 1), scale, reach)
        joined_ref[s] = jnp.where(reach < LANES, first, second)
        turned_ref[s] = second


def stack_kernel(
    chip_ref, next_ref, placed_ref, tail_ref, factor_ref, scale_ref, delay_ref, corner_ref, joined_ref, turned_ref,
    out_ref, frames_ref
):
    components, stations, block = next_ref.shape
    kcount, taps = placed_ref.shape[1:]
    count = block // LANES
    place = lax.axis_index("tm")
    near = (place % 4 == 2).astype(jnp.float32)
    far = (1.0 - near) * (place < lax.axis_size("tm") - 1).astype(jnp.float32)
    arrived = zip(backwards(chip_ref, range(count)), backwards(next_ref, range(count)))
    rows = jnp.concatenate([chip * near + other * far for chip, other in arrived] + [tail_ref[...]], axis=1)
    total = [jnp.zeros((kcount, LANES), jnp.float32) for _ in range(count)]
    for s in range(stations):
        for c in range(components):
            r = c * stations + s
            steps = staircase(rows[r : r + 1, : (count + 1) * LANES], LANES, 1).astype(jnp.bfloat16)
            start = c * TLEN
            frames_ref[s, start : start + LANES, : (count - 1) * LANES] = steps[:, 2 * LANES :]
            frames_ref[s, start : start + LANES, (count - 1) * LANES :] = corner_ref[s, c * LANES : (c + 1) * LANES, :]
            frames_ref[s, start + LANES : start + TLEN, :] = steps[:, LANES:]
    for s in range(stations):
        record_scale = record_scale_of(rows, stations, s, taps)
        correlation = jnp.dot(placed_ref[s], frames_ref[s], preferred_element_type=jnp.float32)
        moveout = delay_ref[s]
        reach = lag(moveout)
        far = moveout >= LANES
        factor = factor_ref[s, 0:1]
        turned = [turned_ref[s]] + [
            turn(block_of(correlation, i), block_of(record_scale, 2 + i), scale_ref[s], reach)
            for i in reversed(range(count))
        ]
        joined = [joined_ref[s]] + [jnp.where(reach < LANES, turned[i], turned[i + 1]) for i in range(count)]
        for i in range(count):
            total[i] = total[i] + jnp.where(far, joined[i + 1], joined[i]) * factor
    out_ref[...] = jnp.concatenate(total, axis=1).astype(jnp.bfloat16).reshape(out_ref.shape)


def near_part(own, templates, moveouts, live_mask, owner_order, gain):
    components, stations, block = own.shape
    kcount, taps = templates.shape[1:]
    row = (stations, kcount, LANES)
    shapes = [
        (templates.shape, jnp.bfloat16), ((-(-components * stations // 8) * 8, 2 * LANES), jnp.float32),
        ((stations, 8, LANES), jnp.float32), (row, jnp.float32), (row, jnp.int32),
        ((stations, taps // 2, LANES), jnp.bfloat16), (row, jnp.float32), (row, jnp.float32),
    ]
    return pl.pallas_call(
        lambda *refs: near_kernel(*refs, gain=gain),
        out_shape=[jax.ShapeDtypeStruct(*shape) for shape in shapes],
        in_specs=[pl.BlockSpec(memory_space=pltpu.HBM)] * 5,
        out_specs=[pl.BlockSpec(memory_space=pltpu.VMEM)] * len(shapes),
        scratch_shapes=[
            pltpu.VMEM(templates.shape, templates.dtype),
            pltpu.VMEM((1, stations), jnp.int32),
            pltpu.VMEM(own.shape, own.dtype),
            pltpu.VMEM(moveouts.shape, moveouts.dtype),
            pltpu.VMEM((1, kcount), jnp.int32),
            pltpu.VMEM((stations, taps, 2 * LANES), jnp.bfloat16),
            pltpu.SemaphoreType.DMA((5,)),
        ],
        compiler_params=pltpu.CompilerParams(vmem_limit_bytes=32 << 20),
        name="near",
    )(*(
        pltpu.with_memory_space_constraint(operand, pltpu.HBM)
        for operand in (live_mask.reshape(1, stations), own, templates, moveouts, owner_order.reshape(1, kcount))
    ))


def stack_part(ahead, near, groups):
    components, stations, block = ahead[0].shape
    kcount, taps = near[0].shape[1:]
    vmem = pl.BlockSpec(memory_space=pltpu.VMEM)
    return pl.pallas_call(
        stack_kernel,
        out_shape=jax.ShapeDtypeStruct((groups, kcount // groups, block), jnp.bfloat16),
        in_specs=[vmem] * (len(ahead) + len(near)),
        out_specs=vmem,
        scratch_shapes=[pltpu.VMEM((stations, taps, block), jnp.bfloat16)],
        compiler_params=pltpu.CompilerParams(vmem_limit_bytes=32 << 20),
        name="stack",
    )(*ahead, *near)


def swapped(count):
    return [(i, i ^ 1) for i in range(count)]


def backward(count):
    pairs = {i: i - 1 for i in range(1, count)}
    pairs.update({i: i + 3 for i in range(3, count - 5, 4)})
    pairs.update({0: 2, count - 5: count - 1})
    return list(pairs.items())


def shards(record, templates, moveouts, live_mask, owner_order):
    stations, components = record.shape[:2]
    count = lax.axis_size("tm")
    groups = lax.axis_size("sta")
    own = jnp.transpose(record, (1, 0, 2))
    ahead = (lax.ppermute(own, "tm", swapped(count)), lax.ppermute(own, "tm", backward(count)))
    gain = math.sqrt(components * TLEN / (stations * groups))
    near = near_part(own, templates, moveouts, live_mask, owner_order, gain)
    partial = stack_part(ahead, near, groups)
    parts = lax.all_to_all(partial, "sta", 0, 0)
    return jnp.sum(parts.astype(jnp.float32), axis=0)


def solution(mesh):
    placed = (P("sta", None, "tm"), P("sta", None, None), P("sta", None), P("sta"), P())
    return jax.shard_map(
        shards, mesh=mesh, in_specs=placed, out_specs=P("sta", "tm"), check_vma=False
    )
```

```python
import math

import jax
import jax.numpy as jnp
from jax import lax
from jax.experimental import pallas as pl
from jax.experimental.pallas import tpu as pltpu
from jax.sharding import PartitionSpec as P
TLEN = 256
MAXM = 256
LANES = 128
SPAN = 16
epsilon = 1e-05


def column_of(row, size):
    here = lax.broadcasted_iota(jnp.int32, (size, size), 0)
    there = lax.broadcasted_iota(jnp.int32, (size, size), 1)
    return jnp.sum(jnp.where(here == there, row, jnp.zeros_like(row)), axis=1, keepdims=True)


def block_of(array, i):
    return array[:, i * LANES : (i + 1) * LANES]


def backwards(ref, blocks):
    components, stations = ref.shape[:2]
    rows = jnp.concatenate([ref[c].astype(jnp.float32) for c in range(components)], axis=0)
    rows = jnp.concatenate([rows, jnp.zeros((-rows.shape[0] % 8, rows.shape[1]), jnp.float32)], axis=0)
    mirror = LANES - 1 - lax.broadcasted_iota(jnp.int32, (rows.shape[0], LANES), 1)
    return [jnp.take_along_axis(block_of(rows, i), mirror, axis=1) for i in reversed(blocks)]


def staircase(row, count, step):
    return pltpu.roll(jnp.broadcast_to(row, (count, row.shape[1])), 0, 1, stride=step, stride_axis=0)


def record_scale_of(rows, stations, s, taps):
    squares = sum(jnp.square(rows[r : r + 1]) for r in range(s, taps // TLEN * stations, stations))
    energy = jnp.sum(staircase(squares, SPAN, 1), axis=0, keepdims=True)
    energy = jnp.sum(staircase(energy, LANES // SPAN, SPAN), axis=0, keepdims=True)
    energy = energy + pltpu.roll(energy, LANES, 1)
    return 1.0 / (taps * jnp.sqrt(energy / taps + epsilon))


def lag(moveout):
    return lax.broadcasted_iota(jnp.int32, moveout.shape, 1) + (moveout & (LANES - 1))


def turn(correlation, record_scale, template_scale, reach):
    score = (correlation * record_scale * template_scale).astype(jnp.bfloat16).astype(jnp.float32)
    return jnp.take_along_axis(score, LANES - 1 - (reach & (LANES - 1)), axis=1)


def near_kernel(
    live_hbm, own_hbm, template_hbm, moveout_hbm, order_hbm,
    placed_ref, tail_ref, factor_ref, scale_ref, delay_ref, corner_ref, joined_ref, turned_ref,
    template_ref, live_ref, own_ref, moveout_ref, order_ref, frames_ref, sems, *, gain
):
    components, stations, block = own_ref.shape
    kcount, taps = template_ref.shape[1:]
    pairs = [
        (own_hbm, own_ref), (moveout_hbm, moveout_ref), (order_hbm, order_ref), (live_hbm, live_ref),
        (template_hbm, template_ref),
    ]
    copies = [pltpu.make_async_copy(*pair, sems.at[i]) for i, pair in enumerate(pairs)]
    for copy in copies[:1] + copies[2:3] + copies[-1:] + copies[1:2] + copies[3:4]:
        copy.start()
    copies[0].wait()
    copies[2].wait()
    blocks = backwards(own_ref, range(block // LANES))
    rows = jnp.concatenate(blocks, axis=1)
    last = block // LANES - 1
    for i in range(2):
        tail_ref[:, i * LANES : (i + 1) * LANES] = blocks[i]
    for s in range(stations):
        for c in range(components):
            r = c * stations + s
            steps = staircase(rows[r : r + 1], LANES, 1).astype(jnp.bfloat16)
            corner_ref[s, c * LANES : (c + 1) * LANES, :] = block_of(steps, last - 2)
            for h in range(TLEN // LANES):
                start = c * TLEN + h * LANES
                frames_ref[s, start : start + LANES, :] = steps[:, (last - 1 - h) * LANES : (last + 1 - h) * LANES]
    order = column_of(order_ref[...], kcount)
    chosen = (order == lax.broadcasted_iota(jnp.int32, (kcount, kcount), 1)).astype(jnp.bfloat16)
    for copy in (copies[1], copies[3], copies[4]):
        copy.wait()
    delays = lax.dot_general(
        chosen, moveout_ref[...].astype(jnp.bfloat16), (((1,), (1,)), ((), ())), preferred_element_type=jnp.float32
    ).astype(jnp.int32)
    for s in range(stations):
        delay_ref[s] = jnp.broadcast_to(delays[:, s : s + 1], (kcount, LANES))
        factor_ref[s] = jnp.broadcast_to(live_ref[0:1, s : s + 1].astype(jnp.float32) * gain, (8, LANES))
    for s in range(stations):
        record_scale = record_scale_of(rows, stations, s, taps)
        wide = jnp.dot(chosen, template_ref[s], preferred_element_type=jnp.float32)
        placed_ref[s] = wide.astype(jnp.bfloat16)
        energy = jnp.sum(wide * wide, axis=1, keepdims=True)
        scale = jnp.broadcast_to(1.0 / jnp.sqrt(energy / taps + epsilon), (kcount, LANES))
        scale_ref[s] = scale
        correlation = jnp.dot(placed_ref[s], frames_ref[s], preferred_element_type=jnp.float32)
        reach = lag(delay_ref[s])
        first = turn(block_of(correlation, 1), block_of(record_scale, last), scale, reach)
        second = turn(block_of(correlation, 0), block_of(record_scale, last - 1), scale, reach)
        joined_ref[s] = jnp.where(reach < LANES, first, second)
        turned_ref[s] = second


def stack_kernel(
    next_ref, chip_ref, placed_ref, tail_ref, factor_ref, scale_ref, delay_ref, corner_ref, joined_ref, turned_ref,
    out_ref, frames_ref
):
    components, stations, block = next_ref.shape
    kcount, taps = placed_ref.shape[1:]
    count = block // LANES
    place = lax.axis_index("tm")
    near = (place % 4 == 0).astype(jnp.float32)
    far = (1.0 - near) * (place < lax.axis_size("tm") - 1).astype(jnp.float32)
    arrived = zip(backwards(chip_ref, range(count)), backwards(next_ref, range(count)))
    rows = jnp.concatenate([chip * near + other * far for chip, other in arrived] + [tail_ref[...]], axis=1)
    total = [jnp.zeros((kcount, LANES), jnp.float32) for _ in range(count)]
    for s in range(stations):
        for c in range(components):
            r = c * stations + s
            steps = staircase(rows[r : r + 1, : (count + 1) * LANES], LANES, 1).astype(jnp.bfloat16)
            start = c * TLEN
            frames_ref[s, start : start + LANES, : (count - 1) * LANES] = steps[:, 2 * LANES :]
            frames_ref[s, start : start + LANES, (count - 1) * LANES :] = corner_ref[s, c * LANES : (c + 1) * LANES, :]
            frames_ref[s, start + LANES : start + TLEN, :] = steps[:, LANES:]
    for s in range(stations):
        record_scale = record_scale_of(rows, stations, s, taps)
        correlation = jnp.dot(placed_ref[s], frames_ref[s], preferred_element_type=jnp.float32)
        moveout = delay_ref[s]
        reach = lag(moveout)
        far = moveout >= LANES
        factor = factor_ref[s, 0:1]
        turned = [turned_ref[s]] + [
            turn(block_of(correlation, i), block_of(record_scale, 2 + i), scale_ref[s], reach)
            for i in reversed(range(count))
        ]
        joined = [joined_ref[s]] + [jnp.where(reach < LANES, turned[i], turned[i + 1]) for i in range(count)]
        for i in range(count):
            total[i] = total[i] + jnp.where(far, joined[i + 1], joined[i]) * factor
    out_ref[...] = jnp.concatenate(total, axis=1).astype(jnp.bfloat16).reshape(out_ref.shape)


def near_part(own, templates, moveouts, live_mask, owner_order, gain):
    components, stations, block = own.shape
    kcount, taps = templates.shape[1:]
    row = (stations, kcount, LANES)
    shapes = [
        (templates.shape, jnp.bfloat16), ((-(-components * stations // 8) * 8, 2 * LANES), jnp.float32),
        ((stations, 8, LANES), jnp.float32), (row, jnp.float32), (row, jnp.int32),
        ((stations, taps // 2, LANES), jnp.bfloat16), (row, jnp.float32), (row, jnp.float32),
    ]
    return pl.pallas_call(
        lambda *refs: near_kernel(*refs, gain=gain),
        out_shape=[jax.ShapeDtypeStruct(*shape) for shape in shapes],
        in_specs=[pl.BlockSpec(memory_space=pltpu.HBM)] * 5,
        out_specs=[pl.BlockSpec(memory_space=pltpu.VMEM)] * len(shapes),
        scratch_shapes=[
            pltpu.VMEM(templates.shape, templates.dtype),
            pltpu.VMEM((1, stations), jnp.int32),
            pltpu.VMEM(own.shape, own.dtype),
            pltpu.VMEM(moveouts.shape, moveouts.dtype),
            pltpu.VMEM((1, kcount), jnp.int32),
            pltpu.VMEM((stations, taps, 2 * LANES), jnp.bfloat16),
            pltpu.SemaphoreType.DMA((5,)),
        ],
        compiler_params=pltpu.CompilerParams(vmem_limit_bytes=32 << 20),
        name="near",
    )(*(
        pltpu.with_memory_space_constraint(operand, pltpu.HBM)
        for operand in (live_mask.reshape(1, stations), own, templates, moveouts, owner_order.reshape(1, kcount))
    ))


def stack_part(ahead, near, groups):
    components, stations, block = ahead[0].shape
    kcount, taps = near[0].shape[1:]
    vmem = pl.BlockSpec(memory_space=pltpu.VMEM)
    return pl.pallas_call(
        stack_kernel,
        out_shape=jax.ShapeDtypeStruct((groups, kcount // groups, block), jnp.bfloat16),
        in_specs=[vmem] * (len(ahead) + len(near)),
        out_specs=vmem,
        scratch_shapes=[pltpu.VMEM((stations, taps, block), jnp.bfloat16)],
        compiler_params=pltpu.CompilerParams(vmem_limit_bytes=32 << 20),
        name="stack",
    )(*ahead, *near)


def swapped(count):
    return [(i, i ^ 1) for i in range(count)]


def backward(count):
    pairs = {i: i - 1 for i in range(1, count)}
    pairs.update({i: i + 3 for i in range(5, count - 3, 4)})
    pairs.update({0: 4, count - 3: count - 1})
    return list(pairs.items())


def shards(record, templates, moveouts, live_mask, owner_order):
    stations, components = record.shape[:2]
    count = lax.axis_size("tm")
    groups = lax.axis_size("sta")
    own = jnp.transpose(record, (1, 0, 2))
    ahead = (lax.ppermute(own, "tm", backward(count)), lax.ppermute(own, "tm", swapped(count)))
    gain = math.sqrt(components * TLEN / (stations * groups))
    near = near_part(own, templates, moveouts, live_mask, owner_order, gain)
    partial = stack_part(ahead, near, groups)
    parts = lax.all_to_all(partial, "sta", 0, 0)
    return jnp.sum(parts.astype(jnp.float32), axis=0)


def solution(mesh):
    placed = (P("sta", None, "tm"), P("sta", None, None), P("sta", None), P("sta"), P())
    return jax.shard_map(
        shards, mesh=mesh, in_specs=placed, out_specs=P("sta", "tm"), check_vma=False
    )
```

```python
import math

import jax
import jax.numpy as jnp
from jax import lax
from jax.experimental import pallas as pl
from jax.experimental.pallas import tpu as pltpu
from jax.sharding import PartitionSpec as P
TLEN = 256
MAXM = 256
LANES = 128
SPAN = 16
epsilon = 1e-05


def column_of(row, size):
    here = lax.broadcasted_iota(jnp.int32, (size, size), 0)
    there = lax.broadcasted_iota(jnp.int32, (size, size), 1)
    return jnp.sum(jnp.where(here == there, row, jnp.zeros_like(row)), axis=1, keepdims=True)


def block_of(array, i):
    return array[:, i * LANES : (i + 1) * LANES]


def backwards(ref, blocks):
    components, stations = ref.shape[:2]
    rows = jnp.concatenate([ref[c].astype(jnp.float32) for c in range(components)], axis=0)
    rows = jnp.concatenate([rows, jnp.zeros((-rows.shape[0] % 8, rows.shape[1]), jnp.float32)], axis=0)
    mirror = LANES - 1 - lax.broadcasted_iota(jnp.int32, (rows.shape[0], LANES), 1)
    return [jnp.take_along_axis(block_of(rows, i), mirror, axis=1) for i in reversed(blocks)]


def staircase(row, count, step):
    return pltpu.roll(jnp.broadcast_to(row, (count, row.shape[1])), 0, 1, stride=step, stride_axis=0)


def record_scale_of(rows, stations, s, taps):
    squares = sum(jnp.square(rows[r : r + 1]) for r in range(s, taps // TLEN * stations, stations))
    energy = jnp.sum(staircase(squares, SPAN, 1), axis=0, keepdims=True)
    energy = jnp.sum(staircase(energy, LANES // SPAN, SPAN), axis=0, keepdims=True)
    energy = energy + pltpu.roll(energy, LANES, 1)
    return 1.0 / (taps * jnp.sqrt(energy / taps + epsilon))


def lag(moveout):
    return lax.broadcasted_iota(jnp.int32, moveout.shape, 1) + (moveout & (LANES - 1))


def turn(correlation, record_scale, template_scale, reach):
    score = (correlation * record_scale * template_scale).astype(jnp.bfloat16).astype(jnp.float32)
    return jnp.take_along_axis(score, LANES - 1 - (reach & (LANES - 1)), axis=1)


def near_kernel(
    live_hbm, own_hbm, template_hbm, moveout_hbm, order_hbm,
    placed_ref, tail_ref, factor_ref, scale_ref, delay_ref, corner_ref, joined_ref, turned_ref,
    template_ref, live_ref, own_ref, moveout_ref, order_ref, frames_ref, sems, *, gain
):
    components, stations, block = own_ref.shape
    kcount, taps = template_ref.shape[1:]
    pairs = [
        (own_hbm, own_ref), (moveout_hbm, moveout_ref), (order_hbm, order_ref), (live_hbm, live_ref),
        (template_hbm, template_ref),
    ]
    copies = [pltpu.make_async_copy(*pair, sems.at[i]) for i, pair in enumerate(pairs)]
    for copy in copies[:1] + copies[2:3] + copies[-1:] + copies[1:2] + copies[3:4]:
        copy.start()
    copies[0].wait()
    copies[2].wait()
    blocks = backwards(own_ref, range(block // LANES))
    rows = jnp.concatenate(blocks, axis=1)
    last = block // LANES - 1
    for i in range(2):
        tail_ref[:, i * LANES : (i + 1) * LANES] = blocks[i]
    for s in range(stations):
        for c in range(components):
            r = c * stations + s
            steps = staircase(rows[r : r + 1], LANES, 1).astype(jnp.bfloat16)
            corner_ref[s, c * LANES : (c + 1) * LANES, :] = block_of(steps, last - 2)
            for h in range(TLEN // LANES):
                start = c * TLEN + h * LANES
                frames_ref[s, start : start + LANES, :] = steps[:, (last - 1 - h) * LANES : (last + 1 - h) * LANES]
    order = column_of(order_ref[...], kcount)
    chosen = (order == lax.broadcasted_iota(jnp.int32, (kcount, kcount), 1)).astype(jnp.bfloat16)
    for copy in (copies[1], copies[3], copies[4]):
        copy.wait()
    delays = lax.dot_general(
        chosen, moveout_ref[...].astype(jnp.bfloat16), (((1,), (1,)), ((), ())), preferred_element_type=jnp.float32
    ).astype(jnp.int32)
    for s in range(stations):
        delay_ref[s] = jnp.broadcast_to(delays[:, s : s + 1], (kcount, LANES))
        factor_ref[s] = jnp.broadcast_to(live_ref[0:1, s : s + 1].astype(jnp.float32) * gain, (8, LANES))
    for s in range(stations):
        record_scale = record_scale_of(rows, stations, s, taps)
        wide = jnp.dot(chosen, template_ref[s], preferred_element_type=jnp.float32)
        placed_ref[s] = wide.astype(jnp.bfloat16)
        energy = jnp.sum(wide * wide, axis=1, keepdims=True)
        scale = jnp.broadcast_to(1.0 / jnp.sqrt(energy / taps + epsilon), (kcount, LANES))
        scale_ref[s] = scale
        correlation = jnp.dot(placed_ref[s], frames_ref[s], preferred_element_type=jnp.float32)
        reach = lag(delay_ref[s])
        first = turn(block_of(correlation, 1), block_of(record_scale, last), scale, reach)
        second = turn(block_of(correlation, 0), block_of(record_scale, last - 1), scale, reach)
        joined_ref[s] = jnp.where(reach < LANES, first, second)
        turned_ref[s] = second


def stack_kernel(
    chip_ref, next_ref, placed_ref, tail_ref, factor_ref, scale_ref, delay_ref, corner_ref, joined_ref, turned_ref,
    out_ref
):
    components, stations, block = next_ref.shape
    kcount, taps = placed_ref.shape[1:]
    count = block // LANES
    place = lax.axis_index("tm")
    near = (place % 4 == 0).astype(jnp.float32)
    far = (1.0 - near) * (place < lax.axis_size("tm") - 1).astype(jnp.float32)
    arrived = zip(backwards(chip_ref, range(count)), backwards(next_ref, range(count)))
    rows = jnp.concatenate([chip * near + other * far for chip, other in arrived] + [tail_ref[...]], axis=1)
    total = [jnp.zeros((kcount, LANES), jnp.float32) for _ in range(count)]
    for s in range(stations):
        record_scale = record_scale_of(rows, stations, s, taps)
        frames = []
        for c in range(components):
            r = c * stations + s
            steps = staircase(rows[r : r + 1, : (count + 1) * LANES], LANES, 1).astype(jnp.bfloat16)
            corner = corner_ref[s, c * LANES : (c + 1) * LANES, :]
            frames += [jnp.concatenate([steps[:, 2 * LANES :], corner], axis=1), steps[:, LANES:]]
        correlation = jnp.dot(placed_ref[s], jnp.concatenate(frames, axis=0), preferred_element_type=jnp.float32)
        moveout = delay_ref[s]
        reach = lag(moveout)
        far = moveout >= LANES
        factor = factor_ref[s, 0:1]
        turned = [turned_ref[s]] + [
            turn(block_of(correlation, i), block_of(record_scale, 2 + i), scale_ref[s], reach)
            for i in reversed(range(count))
        ]
        joined = [joined_ref[s]] + [jnp.where(reach < LANES, turned[i], turned[i + 1]) for i in range(count)]
        for i in range(count):
            total[i] = total[i] + jnp.where(far, joined[i + 1], joined[i]) * factor
    out_ref[...] = jnp.concatenate(total, axis=1).astype(jnp.bfloat16).reshape(out_ref.shape)


def near_part(own, templates, moveouts, live_mask, owner_order, gain):
    components, stations, block = own.shape
    kcount, taps = templates.shape[1:]
    row = (stations, kcount, LANES)
    shapes = [
        (templates.shape, jnp.bfloat16), ((-(-components * stations // 8) * 8, 2 * LANES), jnp.float32),
        ((stations, 8, LANES), jnp.float32), (row, jnp.float32), (row, jnp.int32),
        ((stations, taps // 2, LANES), jnp.bfloat16), (row, jnp.float32), (row, jnp.float32),
    ]
    return pl.pallas_call(
        lambda *refs: near_kernel(*refs, gain=gain),
        out_shape=[jax.ShapeDtypeStruct(*shape) for shape in shapes],
        in_specs=[pl.BlockSpec(memory_space=pltpu.HBM)] * 5,
        out_specs=[pl.BlockSpec(memory_space=pltpu.VMEM)] * len(shapes),
        scratch_shapes=[
            pltpu.VMEM(templates.shape, templates.dtype),
            pltpu.VMEM((1, stations), jnp.int32),
            pltpu.VMEM(own.shape, own.dtype),
            pltpu.VMEM(moveouts.shape, moveouts.dtype),
            pltpu.VMEM((1, kcount), jnp.int32),
            pltpu.VMEM((stations, taps, 2 * LANES), jnp.bfloat16),
            pltpu.SemaphoreType.DMA((5,)),
        ],
        compiler_params=pltpu.CompilerParams(vmem_limit_bytes=32 << 20),
        name="near",
    )(*(
        pltpu.with_memory_space_constraint(operand, pltpu.HBM)
        for operand in (live_mask.reshape(1, stations), own, templates, moveouts, owner_order.reshape(1, kcount))
    ))


def stack_part(ahead, near, groups):
    components, stations, block = ahead[0].shape
    kcount, taps = near[0].shape[1:]
    vmem = pl.BlockSpec(memory_space=pltpu.VMEM)
    return pl.pallas_call(
        stack_kernel,
        out_shape=jax.ShapeDtypeStruct((groups, kcount // groups, block), jnp.bfloat16),
        in_specs=[vmem] * (len(ahead) + len(near)),
        out_specs=vmem,
        compiler_params=pltpu.CompilerParams(vmem_limit_bytes=32 << 20),
        name="stack",
    )(*ahead, *near)


def swapped(count):
    return [(i, i ^ 1) for i in range(count)]


def backward(count):
    pairs = {i: i - 1 for i in range(1, count)}
    pairs.update({i: i + 3 for i in range(5, count - 3, 4)})
    pairs.update({0: 4, count - 3: count - 1})
    return list(pairs.items())


def shards(record, templates, moveouts, live_mask, owner_order):
    stations, components = record.shape[:2]
    count = lax.axis_size("tm")
    groups = lax.axis_size("sta")
    own = jnp.transpose(record, (1, 0, 2))
    ahead = (lax.ppermute(own, "tm", swapped(count)), lax.ppermute(own, "tm", backward(count)))
    gain = math.sqrt(components * TLEN / (stations * groups))
    near = near_part(own, templates, moveouts, live_mask, owner_order, gain)
    partial = stack_part(ahead, near, groups)
    parts = lax.all_to_all(partial, "sta", 0, 0)
    return jnp.sum(parts.astype(jnp.float32), axis=0)


def solution(mesh):
    placed = (P("sta", None, "tm"), P("sta", None, None), P("sta", None), P("sta"), P())
    return jax.shard_map(
        shards, mesh=mesh, in_specs=placed, out_specs=P("sta", "tm"), check_vma=False
    )
```

```python
import math

import jax
import jax.numpy as jnp
from jax import lax
from jax.experimental import pallas as pl
from jax.experimental.pallas import tpu as pltpu
from jax.sharding import PartitionSpec as P
TLEN = 256
MAXM = 256
LANES = 128
SPAN = 16
epsilon = 1e-05


def column_of(row, size):
    here = lax.broadcasted_iota(jnp.int32, (size, size), 0)
    there = lax.broadcasted_iota(jnp.int32, (size, size), 1)
    return jnp.sum(jnp.where(here == there, row, jnp.zeros_like(row)), axis=1, keepdims=True)


def block_of(array, i):
    return array[:, i * LANES : (i + 1) * LANES]


def backwards(ref, blocks):
    components, stations = ref.shape[:2]
    rows = jnp.concatenate([ref[c].astype(jnp.float32) for c in range(components)], axis=0)
    rows = jnp.concatenate([rows, jnp.zeros((-rows.shape[0] % 8, rows.shape[1]), jnp.float32)], axis=0)
    mirror = LANES - 1 - lax.broadcasted_iota(jnp.int32, (rows.shape[0], LANES), 1)
    return [jnp.take_along_axis(block_of(rows, i), mirror, axis=1) for i in reversed(blocks)]


def staircase(row, count, step):
    return pltpu.roll(jnp.broadcast_to(row, (count, row.shape[1])), 0, 1, stride=step, stride_axis=0)


def record_scale_of(rows, stations, s, taps):
    squares = sum(jnp.square(rows[r : r + 1]) for r in range(s, taps // TLEN * stations, stations))
    energy = jnp.sum(staircase(squares, SPAN, 1), axis=0, keepdims=True)
    energy = jnp.sum(staircase(energy, LANES // SPAN, SPAN), axis=0, keepdims=True)
    energy = energy + pltpu.roll(energy, LANES, 1)
    return 1.0 / (taps * jnp.sqrt(energy / taps + epsilon))


def lag(moveout):
    return lax.broadcasted_iota(jnp.int32, moveout.shape, 1) + (moveout & (LANES - 1))


def turn(correlation, record_scale, template_scale, reach):
    score = (correlation * record_scale * template_scale).astype(jnp.bfloat16).astype(jnp.float32)
    return jnp.take_along_axis(score, LANES - 1 - (reach & (LANES - 1)), axis=1)


def near_kernel(
    live_hbm, own_hbm, template_hbm, moveout_hbm, order_hbm,
    placed_ref, tail_ref, factor_ref, scale_ref, delay_ref, corner_ref, joined_ref, turned_ref,
    template_ref, live_ref, own_ref, moveout_ref, order_ref, frames_ref, sems, *, gain
):
    components, stations, block = own_ref.shape
    kcount, taps = template_ref.shape[1:]
    pairs = [
        (own_hbm, own_ref), (moveout_hbm, moveout_ref), (order_hbm, order_ref), (live_hbm, live_ref),
        (template_hbm, template_ref),
    ]
    copies = [pltpu.make_async_copy(*pair, sems.at[i]) for i, pair in enumerate(pairs)]
    for copy in copies[:1] + copies[2:3] + copies[-1:] + copies[1:2] + copies[3:4]:
        copy.start()
    copies[0].wait()
    copies[2].wait()
    blocks = backwards(own_ref, range(block // LANES))
    rows = jnp.concatenate(blocks, axis=1)
    last = block // LANES - 1
    for i in range(2):
        tail_ref[:, i * LANES : (i + 1) * LANES] = blocks[i]
    for s in range(stations):
        for c in range(components):
            r = c * stations + s
            steps = staircase(rows[r : r + 1], LANES, 1).astype(jnp.bfloat16)
            corner_ref[s, c * LANES : (c + 1) * LANES, :] = block_of(steps, last - 2)
            for h in range(TLEN // LANES):
                start = c * TLEN + h * LANES
                frames_ref[s, start : start + LANES, :] = steps[:, (last - 1 - h) * LANES : (last + 1 - h) * LANES]
    order = column_of(order_ref[...], kcount)
    chosen = (order == lax.broadcasted_iota(jnp.int32, (kcount, kcount), 1)).astype(jnp.bfloat16)
    for copy in (copies[1], copies[3], copies[4]):
        copy.wait()
    delays = lax.dot_general(
        chosen, moveout_ref[...].astype(jnp.bfloat16), (((1,), (1,)), ((), ())), preferred_element_type=jnp.float32
    ).astype(jnp.int32)
    for s in range(stations):
        delay_ref[s] = jnp.broadcast_to(delays[:, s : s + 1], (kcount, LANES))
        factor_ref[s] = jnp.broadcast_to(live_ref[0:1, s : s + 1].astype(jnp.float32) * gain, (8, LANES))
    wides = [jnp.dot(chosen, template_ref[s], preferred_element_type=jnp.float32) for s in range(stations)]
    for s in range(stations):
        record_scale = record_scale_of(rows, stations, s, taps)
        wide = wides[s]
        placed = wide.astype(jnp.bfloat16)
        placed_ref[s] = placed
        energy = jnp.sum(wide * wide, axis=1, keepdims=True)
        scale = jnp.broadcast_to(1.0 / jnp.sqrt(energy / taps + epsilon), (kcount, LANES))
        scale_ref[s] = scale
        correlation = jnp.dot(placed, frames_ref[s], preferred_element_type=jnp.float32)
        reach = lag(delay_ref[s])
        first = turn(block_of(correlation, 1), block_of(record_scale, last), scale, reach)
        second = turn(block_of(correlation, 0), block_of(record_scale, last - 1), scale, reach)
        joined_ref[s] = jnp.where(reach < LANES, first, second)
        turned_ref[s] = second


def stack_kernel(
    chip_ref, next_ref, placed_ref, tail_ref, factor_ref, scale_ref, delay_ref, corner_ref, joined_ref, turned_ref,
    out_ref, frames_ref
):
    components, stations, block = next_ref.shape
    kcount, taps = placed_ref.shape[1:]
    count = block // LANES
    place = lax.axis_index("tm")
    near = (place % 4 == 0).astype(jnp.float32)
    far = (1.0 - near) * (place < lax.axis_size("tm") - 1).astype(jnp.float32)
    arrived = zip(backwards(chip_ref, range(count)), backwards(next_ref, range(count)))
    rows = jnp.concatenate([chip * near + other * far for chip, other in arrived] + [tail_ref[...]], axis=1)
    total = [jnp.zeros((kcount, LANES), jnp.float32) for _ in range(count)]
    for s in range(stations):
        for c in range(components):
            r = c * stations + s
            steps = staircase(rows[r : r + 1, : (count + 1) * LANES], LANES, 1).astype(jnp.bfloat16)
            start = c * TLEN
            frames_ref[s, start : start + LANES, : (count - 1) * LANES] = steps[:, 2 * LANES :]
            frames_ref[s, start : start + LANES, (count - 1) * LANES :] = corner_ref[s, c * LANES : (c + 1) * LANES, :]
            frames_ref[s, start + LANES : start + TLEN, :] = steps[:, LANES:]
    for s in range(stations):
        record_scale = record_scale_of(rows, stations, s, taps)
        correlation = jnp.dot(placed_ref[s], frames_ref[s], preferred_element_type=jnp.float32)
        moveout = delay_ref[s]
        reach = lag(moveout)
        far = moveout >= LANES
        factor = factor_ref[s, 0:1]
        turned = [turned_ref[s]] + [
            turn(block_of(correlation, i), block_of(record_scale, 2 + i), scale_ref[s], reach)
            for i in reversed(range(count))
        ]
        joined = [joined_ref[s]] + [jnp.where(reach < LANES, turned[i], turned[i + 1]) for i in range(count)]
        for i in range(count):
            total[i] = total[i] + jnp.where(far, joined[i + 1], joined[i]) * factor
    out_ref[...] = jnp.concatenate(total, axis=1).astype(jnp.bfloat16).reshape(out_ref.shape)


def near_part(own, templates, moveouts, live_mask, owner_order, gain):
    components, stations, block = own.shape
    kcount, taps = templates.shape[1:]
    row = (stations, kcount, LANES)
    shapes = [
        (templates.shape, jnp.bfloat16), ((-(-components * stations // 8) * 8, 2 * LANES), jnp.float32),
        ((stations, 8, LANES), jnp.float32), (row, jnp.float32), (row, jnp.int32),
        ((stations, taps // 2, LANES), jnp.bfloat16), (row, jnp.float32), (row, jnp.float32),
    ]
    return pl.pallas_call(
        lambda *refs: near_kernel(*refs, gain=gain),
        out_shape=[jax.ShapeDtypeStruct(*shape) for shape in shapes],
        in_specs=[pl.BlockSpec(memory_space=pltpu.HBM)] * 5,
        out_specs=[pl.BlockSpec(memory_space=pltpu.VMEM)] * len(shapes),
        scratch_shapes=[
            pltpu.VMEM(templates.shape, templates.dtype),
            pltpu.VMEM((1, stations), jnp.int32),
            pltpu.VMEM(own.shape, own.dtype),
            pltpu.VMEM(moveouts.shape, moveouts.dtype),
            pltpu.VMEM((1, kcount), jnp.int32),
            pltpu.VMEM((stations, taps, 2 * LANES), jnp.bfloat16),
            pltpu.SemaphoreType.DMA((5,)),
        ],
        compiler_params=pltpu.CompilerParams(vmem_limit_bytes=32 << 20),
        name="near",
    )(*(
        pltpu.with_memory_space_constraint(operand, pltpu.HBM)
        for operand in (live_mask.reshape(1, stations), own, templates, moveouts, owner_order.reshape(1, kcount))
    ))


def stack_part(ahead, near, groups):
    components, stations, block = ahead[0].shape
    kcount, taps = near[0].shape[1:]
    vmem = pl.BlockSpec(memory_space=pltpu.VMEM)
    return pl.pallas_call(
        stack_kernel,
        out_shape=jax.ShapeDtypeStruct((groups, kcount // groups, block), jnp.bfloat16),
        in_specs=[vmem] * (len(ahead) + len(near)),
        out_specs=vmem,
        scratch_shapes=[pltpu.VMEM((stations, taps, block), jnp.bfloat16)],
        compiler_params=pltpu.CompilerParams(vmem_limit_bytes=32 << 20),
        name="stack",
    )(*ahead, *near)


def swapped(count):
    return [(i, i ^ 1) for i in range(count)]


def backward(count):
    pairs = {i: i - 1 for i in range(1, count)}
    pairs.update({i: i + 3 for i in range(5, count - 3, 4)})
    pairs.update({0: 4, count - 3: count - 1})
    return list(pairs.items())


def shards(record, templates, moveouts, live_mask, owner_order):
    stations, components = record.shape[:2]
    count = lax.axis_size("tm")
    groups = lax.axis_size("sta")
    own = jnp.transpose(record, (1, 0, 2))
    ahead = (lax.ppermute(own, "tm", swapped(count)), lax.ppermute(own, "tm", backward(count)))
    gain = math.sqrt(components * TLEN / (stations * groups))
    near = near_part(own, templates, moveouts, live_mask, owner_order, gain)
    partial = stack_part(ahead, near, groups)
    parts = lax.all_to_all(partial, "sta", 0, 0)
    return jnp.sum(parts.astype(jnp.float32), axis=0)


def solution(mesh):
    placed = (P("sta", None, "tm"), P("sta", None, None), P("sta", None), P("sta"), P())
    return jax.shard_map(
        shards, mesh=mesh, in_specs=placed, out_specs=P("sta", "tm"), check_vma=False
    )
```
